1024 devices in a mesh: seq: 32 (over z, core), exp: 4 (over x), ch: 8 (over y).
Axes of the slice: x: 4, y: 8, z: 16, core: 2. Of those that a mesh axis runs over, the one named last changes fastest.
Arguments:
- conv_x: bfloat16 [4096, 8192], P('seq', ('exp', 'ch')), may hold values from -6 to 6
- gate_z: bfloat16 [4096, 8192], P('seq', ('exp', 'ch')), may hold values from -6 to 6
- step: bfloat16 [4096, 8192], P('seq', ('exp', 'ch')), may hold values from 0 to 40962
- decay_rate: float32 [8192], P(('exp', 'ch')), may hold values from 0 to 1
- state_in: float32 [4096, 16], P('seq'), may hold values from -6 to 6
- state_out: float32 [4096, 16], P('seq'), may hold values from -6 to 6
- skip: float32 [8192], P(('exp', 'ch')), may hold values from 0.5 to 1.5
- out_weight: bfloat16 [8192, 4096], P(('exp', 'ch')), may hold values from -0.125 to 0.125
- residual: bfloat16 [4096, 4096], P('seq'), may hold values from -6 to 6
- norm_gain: float32 [4096], replicated, may hold values from 0.25 to 1.75
- expert_ids: int32 [4096, 2], P('seq'), may hold values from 0 to 15, all different within a row; in each aligned block of 128 rows (0 to 127, 128 to 255, ...) at most 18 rows name the same one
- expert_weights: bfloat16 [32, 1, 4096, 8, 1536], P('seq', None, 'exp', 'ch'), may hold values from -0.09375 to 0.09375
Outputs:
- expert_hidden: bfloat16 [32, 576, 1, 6144], P('seq', 'exp', None, 'ch')
The draws below stay inside these ranges and needn't reach their ends.
Inputs may be any that keep to these rules, and one draw needn't show every extreme that they name: `expert_ids`: each token names 2 different experts. In each block of 128 tokens (the tokens of one index of seq) no expert is named more than 18 times, a bound that some block reaches.
All inputs are finite; a program needn't handle non-finite values.
Results may differ from the reference program's by a relative error of at most 0.03.
Values may be sent and summed in bfloat16 or wider, within the bound.
A program may use at most 32 MiB of HBM per device.

```python
import math
import jax
import jax.numpy as jnp
import numpy as np
from jax import lax

D = 4096
INNER_CHANNELS = 8192
STATE = 16
EXPERTS = 16
TOP = 2
BLOCK = 32
JUMP_POSITIONS = 3
TOK_SEQ = 128
TOKEN_TOTAL = 4096
CAP = 18
EXP_SEQ = 1
GROUPS = 16
FFB = 768
N_SEQ = 32
N_EXP = 4
N_CH = 8


def channel_rates(key):
    base_key = jax.random.fold_in(key, 7)
    kind_key, fast_key, slow_key = jax.random.split(base_key, 3)
    channel_kind = jax.random.randint(kind_key, (INNER_CHANNELS,), 0, 16)
    fast_mask = channel_kind < 8
    fast_rate = jnp.exp(jax.random.uniform(fast_key, (INNER_CHANNELS,), jnp.float32, math.log(1.0 / 50.0), math.log(1.0 / 25.0)))
    slow_rate = jnp.exp(jax.random.uniform(slow_key, (INNER_CHANNELS,), jnp.float32, math.log(0.15), math.log(0.6))) / TOKEN_TOTAL
    return jnp.where(fast_mask, fast_rate, slow_rate)


def draw_decay_rate(key, part):
    return channel_rates(key)


def draw_step(key, part):
    current_rates = channel_rates(key)
    step_key = jax.random.fold_in(key, 29)
    base_key, location_key, loss_random_key = jax.random.split(step_key, 3)
    baseline_step = jax.random.uniform(base_key, (TOKEN_TOTAL, INNER_CHANNELS), jnp.float32, 0.5, 1.5)
    jump_locations = jax.random.randint(location_key, (JUMP_POSITIONS,), 0, TOKEN_TOTAL)
    jump_losses = jax.random.uniform(loss_random_key, (JUMP_POSITIONS, INNER_CHANNELS), jnp.float32, 0.2, 0.5)
    jump_rows = (jnp.arange(TOKEN_TOTAL)[:, None] == jump_locations[None, :]).astype(jnp.float32)
    grand_total = baseline_step + jnp.dot(jump_rows, jump_losses / current_rates[None, :], precision=lax.Precision.HIGHEST)
    return grand_total.astype(jnp.bfloat16)


def spiked(result, own_key, source, target, shards_of, factor):
    def block_of(axis_at):
        return (jnp.arange(result.shape[axis_at]) // (result.shape[axis_at] // shards_of)).reshape((-1,) + (1,) * (result.ndim - 1 - axis_at))

    first = jax.random.permutation(own_key, shards_of)[block_of(target)]
    far = (block_of(target) + shards_of // 2) % shards_of
    return jnp.where((block_of(source) == first) | (block_of(source) == far), factor * result, result)


def level_of(key, shape, cuts, smallest, top_value):
    def one(position, shards_of):
        draws = jax.random.uniform(jax.random.fold_in(jax.random.fold_in(key, 6), position), (shards_of,), jnp.float32, smallest / len(cuts), top_value / len(cuts))
        return jnp.repeat(jnp.exp(draws), shape[position] // shards_of).reshape((-1,) + (1,) * (len(shape) - position - 1))

    gain = one(*cuts[0])
    for cut in cuts[1:]:
        gain = gain * one(*cut)
    return gain


def shared_out(stream_key, own, number, rows, number_of, top, reach, skew):
    order = jax.random.permutation(stream_key, number_of)
    heavy_load, usual = shares(number_of, rows * top, reach, skew, True), shares(number_of, rows * top, reach, skew, False)
    places = jnp.arange(number_of)

    def named(tallies, offset_by):
        used = int((tallies > 0).sum())
        fixed = max(1, used // 4)
        moved = fixed + (places - fixed + offset_by * (used - fixed)) % max(1, number_of - fixed)
        return jnp.zeros((number_of,), jnp.int32).at[order[jnp.where(places < fixed, places, moved)]].set(jnp.asarray(tallies, jnp.int32))

    tallies = jnp.where(number % 4 == 0, named(heavy_load, number // 4), named(usual, number - number // 4 - 1))
    mixed = jax.random.permutation(jax.random.fold_in(own, 3), number_of)
    source_of, receiver = mixed[0:number_of // 2 * 2:2], mixed[1:number_of // 2 * 2:2]
    margin = jnp.minimum(tallies[source_of] - 1, reach - tallies[receiver]) // 2
    margin = jnp.where((source_of == order[0]) | (receiver == order[0]) | (tallies[receiver] == 0), 0, jnp.maximum(margin, 0))
    moved = jax.random.randint(jax.random.fold_in(own, 4), (number_of // 2,), 0, 1 << 20) % (margin + 1)
    tallies = tallies.at[source_of].add(-moved).at[receiver].add(moved)
    labels = jnp.searchsorted(jnp.cumsum(tallies), jnp.arange(rows * top), side="right").astype(jnp.int32)
    table = labels.reshape(top, rows).T
    table = table[jax.random.permutation(jax.random.fold_in(own, 1), rows)]
    offset_by = jax.random.randint(jax.random.fold_in(own, 2), (rows, 1), 0, top)
    return jnp.take_along_axis(table, (jnp.arange(top)[None, :] + offset_by) % top, axis=1)


def shares(amount, total, reach, lean, full):
    portions = [(1 << 20) // math.isqrt(rank ** lean) + 1 for rank in range(1, amount + 1)]
    largest = reach if full else min(reach, max(-(-total // amount), total * portions[0] // sum(portions)))
    least = 1 if total - largest >= amount - 1 else 0
    given, spare = [largest] + [least] * (amount - 1), total - largest - least * (amount - 1)
    while spare > 0:
        free = [i for i in range(1, amount) if given[i] < largest] or [i for i in range(1, amount) if given[i] < reach]
        mass, left = sum([portions[i] for i in free]), spare
        for i in free:
            addition = min(reach - given[i], max(1, left * portions[i] // mass), spare)
            given[i] = given[i] + addition
            spare = spare - addition
    return np.array(given)


def normal_values(stream_key, dims, scale, reach, cuts=(), kind=jnp.bfloat16):
    array = jax.random.normal(stream_key, dims, jnp.float32) * scale
    if len(cuts) > 0:
        array = level_of(stream_key, dims, cuts, -0.22, 0.18) * array
    return jnp.clip(array, min=-reach, max=reach).astype(kind)


def heavy_noise(stream_key, dims, scale, bound, cuts, heavy, held_as=jnp.bfloat16):
    array = scale * jax.random.normal(stream_key, dims, jnp.float32)
    if cuts:
        array = array * level_of(stream_key, dims, cuts, -0.22, 0.18)
    return jnp.clip(spiked(array, jax.random.fold_in(stream_key, 3), *heavy), -bound, bound).astype(held_as)


def setup_inputs(seed: int = 0) -> dict:
    streams_of = jax.random.split(jax.random.key(seed), 13)
    conv_x = normal_values(streams_of[0], (TOKEN_TOTAL, INNER_CHANNELS), 1.0, 6.0, ((0, 32), (1, 32)))
    gate_z = normal_values(streams_of[1], (TOKEN_TOTAL, INNER_CHANNELS), 1.0, 6.0, ((0, 32), (1, 32)))
    step = draw_step(jax.random.fold_in(streams_of[12], 71), 0)
    decay_rate = draw_decay_rate(jax.random.fold_in(streams_of[12], 71), 0)
    state_in = normal_values(streams_of[4], (TOKEN_TOTAL, STATE), 1.0, 6.0, ((0, 32),), jnp.float32)
    state_out = normal_values(streams_of[5], (TOKEN_TOTAL, STATE), 1.0, 6.0, ((0, 32),), jnp.float32)
    skip = jnp.clip(0.5 + 1.0 * jax.random.uniform(streams_of[6], (INNER_CHANNELS,), jnp.float32) ** level_of(streams_of[6], (INNER_CHANNELS,), ((0, 32),), -0.2, 0.2), 0.5, 1.5)
    out_weight = heavy_noise(streams_of[7], (INNER_CHANNELS, D), INNER_CHANNELS ** -0.5, 0.125, ((0, 32),), (0, 1, 32, 2.75))
    residual = normal_values(streams_of[8], (TOKEN_TOTAL, D), 1.0, 6.0, ((0, 32),))
    norm_gain = jnp.clip(1.0 + 0.15 * jax.random.normal(streams_of[9], (D,), jnp.float32), 0.25, 1.75)
    expert_ids_keys = jax.random.split(jax.random.fold_in(streams_of[10], 1), TOKEN_TOTAL // TOK_SEQ)
    expert_ids_turns = jax.random.permutation(jax.random.fold_in(streams_of[10], 3), TOKEN_TOTAL // TOK_SEQ)
    expert_ids = jax.vmap(lambda own, number: shared_out(jax.random.fold_in(streams_of[10], 2), own, number, TOK_SEQ, EXPERTS, TOP, CAP, 2))(expert_ids_keys, expert_ids_turns).reshape((TOKEN_TOTAL, TOP))
    expert_weights = normal_values(streams_of[11], (N_SEQ, EXP_SEQ, D, N_CH, 2 * FFB), D ** -0.5, 0.09375, ((0, 32), (2, 4), (3, 8)))
    return dict(conv_x=conv_x, gate_z=gate_z, step=step, decay_rate=decay_rate, state_in=state_in, state_out=state_out, skip=skip, out_weight=out_weight, residual=residual, norm_gain=norm_gain, expert_ids=expert_ids, expert_weights=expert_weights)


exact_products = lax.Precision.HIGHEST
norm_epsilon = 1e-05

def block_scan(state_now, block_inputs):
    decay_log, drive_raw, input_mix, output_mix = block_inputs
    length = decay_log.shape[0]
    cumulative = jnp.cumsum(decay_log, axis=0)
    drive_term = jnp.sqrt(-jnp.expm1(-2.0 * decay_log)) * drive_raw
    pairing = jnp.dot(output_mix, input_mix.T, precision=exact_products)
    causal = jnp.arange(length)[:, None] >= jnp.arange(length)[None, :]
    spread = cumulative[:, None, :] - cumulative[None, :, :]
    kernel = jnp.where(causal[:, :, None], jnp.exp(-jnp.where(causal[:, :, None], spread, 0.0)), 0.0)
    within = jnp.einsum('tsc,sc->tc', kernel * pairing[:, :, None], drive_term, precision=exact_products)
    from_before = jnp.exp(-cumulative) * jnp.dot(output_mix, state_now.T, precision=exact_products)
    remaining = jnp.exp(cumulative - cumulative[-1][None, :])
    state_next = jnp.exp(-cumulative[-1])[:, None] * state_now + jnp.dot((remaining * drive_term).T, input_mix, precision=exact_products)
    return (state_next, within + from_before)

def reference(conv_x, gate_z, step, decay_rate, state_in, state_out, skip, out_weight, residual, norm_gain, expert_ids, expert_weights):
    drive_raw = conv_x.astype(jnp.float32)
    decay_log = step.astype(jnp.float32) * decay_rate[None, :]
    block_count = TOKEN_TOTAL // BLOCK
    shaped = (decay_log.reshape(block_count, BLOCK, INNER_CHANNELS), drive_raw.reshape(block_count, BLOCK, INNER_CHANNELS), state_in.reshape(block_count, BLOCK, STATE), state_out.reshape(block_count, BLOCK, STATE))
    initial = jnp.zeros((INNER_CHANNELS, STATE), jnp.float32)
    scanned = lax.scan(block_scan, initial, shaped)[1].reshape(TOKEN_TOTAL, INNER_CHANNELS)
    mamba_out = ((scanned + skip[None, :] * drive_raw) * jax.nn.silu(gate_z.astype(jnp.float32))).astype(jnp.bfloat16)
    mixer_out = jnp.dot(mamba_out, out_weight, preferred_element_type=jnp.float32)
    stream = residual.astype(jnp.float32) + mixer_out
    inverse = lax.rsqrt(lax.optimization_barrier(jnp.mean(stream * stream, axis=1, keepdims=True)) + norm_epsilon)
    normed = (stream * inverse * norm_gain[None, :]).astype(jnp.bfloat16)
    flat_ids = expert_ids.reshape(N_SEQ, TOK_SEQ * TOP).astype(jnp.int32)
    onehot = (flat_ids[:, :, None] == jnp.arange(EXPERTS, dtype=jnp.int32)[None, None, :]).astype(jnp.int32)
    earlier = (jnp.cumsum(onehot, axis=1) - onehot).astype(jnp.int32)
    slot_index = lax.optimization_barrier(jnp.sum(earlier * onehot, axis=2)).astype(jnp.int32)
    source_index = jnp.broadcast_to(jnp.arange(N_SEQ, dtype=jnp.int32)[:, None], flat_ids.shape)
    token_index = jnp.broadcast_to((jnp.arange(TOK_SEQ * TOP, dtype=jnp.int32) // TOP)[None, :], flat_ids.shape)
    slot_table = jnp.full((N_SEQ, EXPERTS, CAP), TOK_SEQ, jnp.int32).at[source_index, flat_ids, slot_index].set(token_index)
    padded = jnp.concatenate([normed.reshape(N_SEQ, TOK_SEQ, D), jnp.zeros((N_SEQ, 1, D), jnp.bfloat16)], axis=1)
    gathered = jnp.take_along_axis(padded, slot_table.reshape(N_SEQ, EXPERTS * CAP)[:, :, None], axis=1)
    gathered = gathered.reshape(N_SEQ, EXPERTS, CAP, D)
    feature_width = D // N_EXP

    def one_owner(owner_inputs):
        owner_index, owner_weights = owner_inputs
        first_expert = (owner_index % GROUPS * EXP_SEQ).astype(jnp.int32)
        row_block = lax.dynamic_slice_in_dim(gathered, first_expert, EXP_SEQ, 1)
        row_block = jnp.transpose(row_block, (0, 2, 1, 3)).reshape(N_SEQ * CAP, EXP_SEQ, N_EXP, feature_width)
        mixing = owner_weights.reshape(EXP_SEQ, N_EXP, feature_width, N_CH * 2 * FFB)
        group_sums = jnp.einsum('rjgi,jgim->rjgm', row_block.astype(jnp.float32), mixing.astype(jnp.float32))
        rounded = lax.optimization_barrier(group_sums.astype(jnp.bfloat16)).astype(jnp.float32)
        summed = lax.optimization_barrier(jnp.sum(rounded, axis=2)).reshape(N_SEQ * CAP, EXP_SEQ, N_CH, 2 * FFB)
        hidden = jax.nn.silu(summed[..., :FFB]) * summed[..., FFB:]
        return hidden.astype(jnp.bfloat16).reshape(N_SEQ * CAP, EXP_SEQ, N_CH * FFB)
    return lax.map(one_owner, (jnp.arange(N_SEQ, dtype=jnp.int32), expert_weights))
```

```python
import functools

import jax
import jax.numpy as jnp
from jax import lax
from jax.experimental import pallas as pl
from jax.experimental.pallas import tpu as pltpu
from jax.sharding import PartitionSpec as P

MESH = pl.DeviceIdType.MESH
F32 = jnp.float32
BF16 = jnp.bfloat16
EXACT = lax.Precision.HIGHEST
EPSILON = 1e-05
MAIN_SLOTS = 16
TAIL_SLOTS = 2
LANES = 128
STATE_GROUP = 4
NX = 4


def silu(v):
    return v / (1.0 + jnp.exp(-v))


def arrived(ref, sem):
    pltpu.make_async_copy(ref, ref, sem).wait()


def send(src, dst, send_sem, recv_sem, device):
    pltpu.make_async_remote_copy(
        src_ref=src,
        dst_ref=dst,
        send_sem=send_sem,
        recv_sem=recv_sem,
        device_id=device,
        device_id_type=MESH,
    ).start()


def kernel(
    nz,
    ny,
    conv_ref,
    gate_ref,
    step_ref,
    rate_ref,
    b_ref,
    c_ref,
    skip_ref,
    gain_ref,
    ids_ref,
    wout_hbm,
    resid_hbm,
    wexp_hbm,
    out_ref,
    wout,
    resid,
    wexp,
    e_ref,
    d_ref,
    y_ref,
    p_ref,
    s1h,
    s1a,
    s2h,
    s2a,
    inc_h,
    inc_a,
    mx_opp,
    mx_r,
    mx_l,
    mx_rc,
    mx_lc,
    mx_own,
    xo_recv,
    xn_recv,
    ysend,
    yrecv,
    zm_send,
    zt_send,
    zm_recv,
    zt_recv,
    ring,
    lhs,
    pb_opp,
    pb_r,
    pb_l,
    pb_rc,
    pb_lc,
    pb_own,
    po_recv,
    pn_recv,
    sq_send,
    sq_recv,
    local_sem,
    s1_ss,
    s1_rs,
    s2_ss,
    s2_rs,
    xo_ss,
    xo_rs,
    xn_ss,
    xn_rs,
    y_ss,
    y_rs,
    zm_ss,
    zm_rs,
    zt_ss,
    zt_rs,
    ring_ss,
    ring_rs,
    po_ss,
    po_rs,
    pn_ss,
    pn_rs,
    sq_ss,
    sq_rs,
):
    s = lax.axis_index("seq")
    x = lax.axis_index("exp")
    y = lax.axis_index("ch")
    tokens, channels = conv_ref.shape
    features = ny * LANES
    half = tokens // 2
    experts = nz // 2
    xr, xl, xo = lax.rem(x + 1, NX), lax.rem(x + 3, NX), lax.rem(x + 2, NX)
    yr, yl = lax.rem(y + 1, ny), lax.rem(y + ny - 1, ny)

    barrier = pltpu.get_barrier_semaphore()

    @pl.loop(1, nz)
    def _(k):
        pl.semaphore_signal(
            barrier, inc=1, device_id={"seq": lax.rem(s + k, nz)}, device_id_type=MESH
        )

    for k in range(1, NX):
        pl.semaphore_signal(
            barrier, inc=1, device_id={"exp": lax.rem(x + k, NX)}, device_id_type=MESH
        )
    for k in range(1, ny):
        pl.semaphore_signal(
            barrier, inc=1, device_id={"ch": lax.rem(y + k, ny)}, device_id_type=MESH
        )

    share = pl.multiple_of((x * ny + y) * LANES, LANES)
    copy_wout = pltpu.make_async_copy(wout_hbm, wout, local_sem.at[0])
    copy_resid = pltpu.make_async_copy(
        resid_hbm.at[:, pl.ds(share, LANES)], resid, local_sem.at[1]
    )
    copy_wexp = pltpu.make_async_copy(wexp_hbm, wexp, local_sem.at[2])
    copy_wout.start()
    copy_resid.start()
    copy_wexp.start()

    def wide(ref):
        return jnp.concatenate(
            [ref[k : k + 1, :] for k in range(channels // LANES)], axis=1
        )

    conv = conv_ref[...].astype(F32)
    decay_log = step_ref[...].astype(F32) * wide(rate_ref)
    decay = jnp.exp(-decay_log)
    twice = 2.0 * decay_log
    series = twice * (
        1.0
        - twice
        * (
            1.0 / 2.0
            - twice
            * (
                1.0 / 6.0
                - twice * (1.0 / 24.0 - twice * (1.0 / 120.0 - twice * (1.0 / 720.0)))
            )
        )
    )
    lost = jnp.where(twice < 0.25, series, 1.0 - jnp.exp(-twice))
    e_ref[...] = decay
    d_ref[...] = jnp.sqrt(lost) * conv

    def eight_tokens(i, carry):
        state, product, b_now, c_now = carry
        rows = pl.ds(pl.multiple_of(i * 8, 8), 8)
        e8 = e_ref[rows, :]
        d8 = d_ref[rows, :]
        outs, products = [], []
        for k in range(8):
            e1 = e8[k : k + 1, :]
            state = e1 * state + d8[k : k + 1, :] * b_now[:, k : k + 1]
            product = product * e1
            outs.append(jnp.sum(state * c_now[:, k : k + 1], axis=0, keepdims=True))
            products.append(product)
        y_ref[rows, :] = jnp.concatenate(outs, axis=0)
        p_ref[rows, :] = jnp.concatenate(products, axis=0)
        shift = b_now.shape[1] - 8
        return state, product, pltpu.roll(b_now, shift, 1), pltpu.roll(c_now, shift, 1)

    state, product, _, _ = lax.fori_loop(
        0,
        tokens // 8,
        eight_tokens,
        (
            jnp.zeros((b_ref.shape[0], channels), F32),
            jnp.ones((1, channels), F32),
            b_ref[...],
            c_ref[...],
        ),
    )

    group, place = s // STATE_GROUP, lax.rem(s, STATE_GROUP)
    groups = nz // STATE_GROUP
    s1h[place] = state.astype(BF16)
    s1a[place] = product
    pl.semaphore_wait(barrier, nz - 1 + NX - 1 + ny - 1)
    for k in range(1, STATE_GROUP):
        other = lax.rem(place + k, STATE_GROUP)
        device = {"seq": group * STATE_GROUP + other}
        send(s1h.at[place], s1h.at[place], s1_ss.at[0, k], s1_rs.at[0, place], device)
        send(s1a.at[place], s1a.at[place], s1_ss.at[1, k], s1_rs.at[1, place], device)
    gates = silu(gate_ref[...].astype(F32))
    within = y_ref[...] + wide(skip_ref) * conv
    for k in range(1, STATE_GROUP):
        other = lax.rem(place + k, STATE_GROUP)
        arrived(s1h.at[other], s1_rs.at[0, other])
        arrived(s1a.at[other], s1_rs.at[1, other])
    total_h = jnp.zeros_like(state)
    total_a = jnp.ones_like(product)
    before_h = jnp.zeros_like(state)
    before_a = jnp.ones_like(product)
    for j in range(STATE_GROUP):
        h_j = s1h[j].astype(F32)
        a_j = s1a[j]
        total_h = a_j * total_h + h_j
        total_a = a_j * total_a
        earlier = j < place
        before_h = jnp.where(earlier, a_j * before_h + h_j, before_h)
        before_a = jnp.where(earlier, a_j * before_a, before_a)
    s2h[group] = total_h.astype(BF16)
    s2a[group] = total_a
    for k in range(groups - 1, 0, -1):

        @pl.when(group + k < groups)
        def _():
            device = {"seq": s + k * STATE_GROUP}
            send(s2h.at[group], s2h.at[group], s2_ss.at[0, k], s2_rs.at[0, group], device)
            send(s2a.at[group], s2a.at[group], s2_ss.at[1, k], s2_rs.at[1, group], device)

    inc_h[...] = jnp.zeros_like(state)
    for j in range(groups - 1):

        @pl.when(j < group)
        def _():
            arrived(s2h.at[j], s2_rs.at[0, j])
            arrived(s2a.at[j], s2_rs.at[1, j])
            inc_h[...] = s2a[j] * inc_h[...] + s2h[j].astype(F32)

    incoming = before_a * inc_h[...] + before_h

    carried = lax.dot_general(
        c_ref[...], incoming, (((0,), (0,)), ((), ())), precision=EXACT,
        preferred_element_type=F32,
    )
    mamba = ((within + p_ref[...] * carried) * gates).astype(BF16)
    copy_wout.wait()

    def project(which, store):
        @pl.loop(0, ny // 2)
        def _(n):
            start = pl.multiple_of(which * features + n * 2 * LANES, 2 * LANES)
            part = jnp.dot(
                mamba, wout[:, pl.ds(start, 2 * LANES)], preferred_element_type=F32
            )
            for h in range(2):
                for j in range(2):
                    store(
                        h,
                        2 * n + j,
                        part[h * half : (h + 1) * half, j * LANES : (j + 1) * LANES],
                    )

    def into_opp(h, n, v):
        mx_opp[h, n] = v.astype(BF16)

    def into_r(h, n, v):
        if h == 0:
            mx_rc[n] = v
        else:
            mx_r[1, n] = v.astype(BF16)

    def into_l(h, n, v):
        if h == 1:
            mx_lc[n] = v
        else:
            mx_l[0, n] = v.astype(BF16)

    def into_own(h, n, v):
        mx_own[h, n] = v

    to_r, to_l = {"exp": xr}, {"exp": xl}
    project(xo, into_opp)
    send(mx_opp.at[0], xo_recv.at[0], xo_ss.at[0], xo_rs.at[0], to_r)
    send(mx_opp.at[1], xo_recv.at[1], xo_ss.at[1], xo_rs.at[1], to_l)
    project(xr, into_r)
    send(mx_r.at[1], xn_recv.at[0, 1], xn_ss.at[0, 1], xn_rs.at[0, 1], to_r)
    project(xl, into_l)
    send(mx_l.at[0], xn_recv.at[1, 0], xn_ss.at[1, 0], xn_rs.at[1, 0], to_l)
    arrived(xo_recv.at[0], xo_rs.at[0])
    mx_r[0] = (mx_rc[...] + xo_recv[0].astype(F32)).astype(BF16)
    send(mx_r.at[0], xn_recv.at[0, 0], xn_ss.at[0, 0], xn_rs.at[0, 0], to_r)
    arrived(xo_recv.at[1], xo_rs.at[1])
    mx_l[1] = (mx_lc[...] + xo_recv[1].astype(F32)).astype(BF16)
    send(mx_l.at[1], xn_recv.at[1, 1], xn_ss.at[1, 1], xn_rs.at[1, 1], to_l)
    project(xo if NX == 1 else x, into_own)

    wide_experts = max(experts, 16)
    names = lax.broadcasted_iota(jnp.int32, (wide_experts, tokens), 0)
    named = (ids_ref[0:1, :] == names) | (ids_ref[1:2, :] == names)
    count = jnp.where(named, 1.0, 0.0)
    before = jnp.where(
        lax.broadcasted_iota(jnp.int32, (tokens, tokens), 0)
        < lax.broadcasted_iota(jnp.int32, (tokens, tokens), 1),
        1.0,
        0.0,
    )
    earlier = jnp.dot(
        count.astype(BF16), before.astype(BF16), preferred_element_type=F32
    )
    slot = jnp.where(named, earlier, -1.0).astype(BF16)

    def picked(slots, first):
        rows = slots * wide_experts
        spread = jnp.where(
            lax.broadcasted_iota(jnp.int32, (rows, wide_experts), 0) // slots
            == lax.broadcasted_iota(jnp.int32, (rows, wide_experts), 1),
            1.0,
            0.0,
        ).astype(BF16)
        per_row = jnp.dot(spread, slot, preferred_element_type=F32)
        wanted = lax.rem(
            lax.broadcasted_iota(jnp.int32, (rows, tokens), 0), slots
        ).astype(F32) + float(first)
        return jnp.where(per_row == wanted, 1.0, 0.0).astype(BF16)

    pick_main = picked(MAIN_SLOTS, 0)
    pick_tail = picked(TAIL_SLOTS, MAIN_SLOTS)

    for side in range(2):
        for h in (1, 0) if side == 0 else (0, 1):
            arrived(xn_recv.at[side, h], xn_rs.at[side, h])
    for n in range(ny):
        for h in range(2):
            ysend[n, h * half : (h + 1) * half, :] = (
                mx_own[h, n]
                + xn_recv[0, h, n].astype(F32)
                + xn_recv[1, h, n].astype(F32)
            ).astype(BF16)
    for k in range(1, ny):
        other = lax.rem(y + k, ny)
        send(ysend.at[other], yrecv.at[y], y_ss.at[k], y_rs.at[y], {"ch": other})
    yrecv[y] = ysend[y]
    for k in range(1, ny):
        other = lax.rem(y + k, ny)
        arrived(yrecv.at[other], y_rs.at[other])
    copy_resid.wait()
    stream = resid[...].astype(F32)
    for n in range(ny):
        stream = stream + yrecv[n].astype(F32)
    rows_of = stream.astype(BF16)

    main_rows = jnp.dot(pick_main, rows_of, preferred_element_type=F32).astype(BF16)
    tail_rows = jnp.dot(pick_tail, rows_of, preferred_element_type=F32)
    zm_send[...] = main_rows.reshape(wide_experts, MAIN_SLOTS, LANES)
    zt_send[...] = tail_rows.reshape(wide_experts, TAIL_SLOTS, LANES)

    def dispatch(owner):
        expert = lax.rem(owner, experts)
        device = {"seq": owner}
        send(zm_send.at[expert], zm_recv.at[s], zm_ss.at[owner], zm_rs.at[s], device)
        send(zt_send.at[expert], zt_recv.at[s], zt_ss.at[owner], zt_rs.at[s], device)

    dispatch(lax.rem(s + nz // 2, nz))

    @pl.loop(1, nz // 2)
    def _(k):
        far = nz // 2 - k
        dispatch(lax.rem(s + far, nz))
        dispatch(lax.rem(s + nz - far, nz))

    mine = lax.rem(s, experts)
    zm_recv[s] = zm_send[mine]
    zt_recv[s] = zt_send[mine]

    blocks = NX
    sources = nz // blocks
    main = sources * MAIN_SLOTS
    tail = sources * TAIL_SLOTS
    order = [xo, xr, xl, x]
    hops = ny // 2
    even = lax.rem(s, 2) == 0

    def fill(k):
        first = order[k] * sources

        @pl.loop(0, sources)
        def _(j):
            @pl.when(first + j != s)
            def _():
                arrived(zm_recv.at[first + j], zm_rs.at[first + j])
                arrived(zt_recv.at[first + j], zt_rs.at[first + j])

        ring[y, k, 0:main, :] = zm_recv[pl.ds(first, sources)].reshape(main, LANES)
        rest = zt_recv[pl.ds(first, sources)].reshape(tail, LANES)
        if tail < 16:
            rest = jnp.concatenate([rest, jnp.zeros((16 - tail, LANES), F32)], axis=0)
        ring[y, k, main:, :] = rest.astype(BF16)

    def hop_right(k, h, first_part):
        held = lax.rem(y + ny - h + 1, ny)
        got = lax.rem(y + ny - h, ny)
        if first_part:
            send(
                ring.at[held, k], ring.at[held, k], ring_ss.at[0, k, h], ring_rs.at[0, k, h],
                {"ch": yr},
            )
        else:
            arrived(ring.at[got, k], ring_rs.at[0, k, h])

    def hop_left(k, h, first_part):
        held = lax.rem(y + h - 1, ny)
        got = lax.rem(y + h, ny)
        if first_part:
            send(
                ring.at[held, k], ring.at[held, k], ring_ss.at[1, k, h], ring_rs.at[1, k, h],
                {"ch": yl},
            )
        else:
            arrived(ring.at[got, k], ring_rs.at[1, k, h])

    def hop(k, h, first_part):
        if h < hops:
            hop_right(k, h, first_part)
            hop_left(k, h, first_part)
        else:

            @pl.when(even)
            def _():
                hop_right(k, h, first_part)

            @pl.when(jnp.logical_not(even))
            def _():
                hop_left(k, h, first_part)

    gated = pb_own.shape[-1]
    width = 256

    def expert_block(k, store):
        squares = jnp.zeros(lhs.shape[:1] + (LANES,), F32)
        for n in range(ny):
            v = ring[n, k].astype(F32)
            squares = squares + v * v
            lhs[:, n * LANES : (n + 1) * LANES] = (
                v * gain_ref[pl.ds(x * ny + n, 1), :]
            ).astype(BF16)
        sq_send[k] = lax.dot_general(
            jnp.ones((8, LANES), F32), squares, (((1,), (1,)), ((), ())),
            precision=EXACT, preferred_element_type=F32,
        )
        for h in range(2):

            @pl.loop(0, gated // width)
            def _(n):
                start = pl.multiple_of(n * width, width)
                part = jnp.dot(
                    lhs[...],
                    wexp[:, pl.ds(h * gated + start, width)],
                    preferred_element_type=F32,
                )
                store(h, pl.ds(start, width), part)

    def keep_opp(h, at, v):
        pb_opp[h, :, at] = v.astype(BF16)

    def keep_r(h, at, v):
        if h == 0:
            pb_rc[:, at] = v
        else:
            pb_r[1, :, at] = v.astype(BF16)

    def keep_l(h, at, v):
        if h == 1:
            pb_lc[:, at] = v
        else:
            pb_l[0, :, at] = v.astype(BF16)

    def keep_own(h, at, v):
        pb_own[h, :, at] = v

    def after_block(k):
        if k == 0:
            expert_block(0, keep_opp)
            send(pb_opp.at[0], po_recv.at[0], po_ss.at[0], po_rs.at[0], to_r)
            send(pb_opp.at[1], po_recv.at[1], po_ss.at[1], po_rs.at[1], to_l)
            send(sq_send.at[0], sq_recv.at[0], sq_ss.at[0], sq_rs.at[0], {"exp": xo})
        elif k == 1:
            expert_block(1, keep_r)
            send(pb_r.at[1], pn_recv.at[0, 1], pn_ss.at[0, 1], pn_rs.at[0, 1], to_r)
            send(sq_send.at[1], sq_recv.at[1], sq_ss.at[1], sq_rs.at[1], to_r)
            arrived(po_recv.at[0], po_rs.at[0])
            pb_r[0] = (pb_rc[...] + po_recv[0].astype(F32)).astype(BF16)
            send(pb_r.at[0], pn_recv.at[0, 0], pn_ss.at[0, 0], pn_rs.at[0, 0], to_r)
        elif k == 2:
            expert_block(2, keep_l)
            send(pb_l.at[0], pn_recv.at[1, 0], pn_ss.at[1, 0], pn_rs.at[1, 0], to_l)
            send(sq_send.at[2], sq_recv.at[2], sq_ss.at[2], sq_rs.at[2], to_l)
            arrived(po_recv.at[1], po_rs.at[1])
            pb_l[1] = (pb_lc[...] + po_recv[1].astype(F32)).astype(BF16)
            send(pb_l.at[1], pn_recv.at[1, 1], pn_ss.at[1, 1], pn_rs.at[1, 1], to_l)
        else:
            expert_block(3, keep_own)

    for turn in range(blocks + hops):
        for k in range(blocks):
            h = turn - k + 1
            if h == 1:
                fill(k)
            if 1 < h <= hops:
                hop(k, h - 1, False)
            if 1 <= h <= hops:
                hop(k, h, True)
        k = turn - hops
        if 0 <= k < blocks:
            hop(k, hops, False)
            if k == 0:
                copy_wexp.wait()
            after_block(k)

    for k in range(3):
        arrived(sq_recv.at[k], sq_rs.at[k])
    sums = sq_send[3] + sq_recv[0] + sq_recv[1] + sq_recv[2]
    inverse = lax.rsqrt(sums / (NX * features) + EPSILON)
    scale = lax.dot_general(
        inverse, jnp.full((8, LANES), 0.125, F32), (((0,), (0,)), ((), ())),
        precision=EXACT, preferred_element_type=F32,
    )[:, 0:1]
    for side in range(2):
        for h in (1, 0) if side == 0 else (0, 1):
            arrived(pn_recv.at[side, h], pn_rs.at[side, h])
    rows = lhs.shape[0]
    slots = MAIN_SLOTS + TAIL_SLOTS
    final = lax.broadcasted_iota(jnp.int32, (sources * slots, rows), 0)
    place_of = lax.broadcasted_iota(jnp.int32, (sources * slots, rows), 1)
    owner_row, slot_row = final // slots, lax.rem(final, slots)
    taken = jnp.where(
        slot_row < MAIN_SLOTS,
        owner_row * MAIN_SLOTS + slot_row,
        main + owner_row * TAIL_SLOTS + slot_row - MAIN_SLOTS,
    )
    arrange = jnp.where(taken == place_of, 1.0, 0.0).astype(BF16)

    @pl.loop(0, gated // width)
    def _(n):
        at = pl.ds(pl.multiple_of(n * width, width), width)
        both = []
        for h in range(2):
            both.append(
                scale
                * (
                    pb_own[h, :, at]
                    + pn_recv[0, h, :, at].astype(F32)
                    + pn_recv[1, h, :, at].astype(F32)
                )
            )
        hidden = (silu(both[0]) * both[1]).astype(BF16)
        out_ref[:, at] = jnp.dot(arrange, hidden, preferred_element_type=F32).astype(BF16)

    for k in range(1, STATE_GROUP):
        arrived(s1h.at[0], s1_ss.at[0, k])
        arrived(s1a.at[0], s1_ss.at[1, k])
    for k in range(1, groups):

        @pl.when(group + k < groups)
        def _():
            arrived(s2h.at[0], s2_ss.at[0, k])
            arrived(s2a.at[0], s2_ss.at[1, k])

    for h in range(2):
        arrived(mx_opp.at[h], xo_ss.at[h])
        arrived(pb_opp.at[h], po_ss.at[h])
        arrived(mx_r.at[h], xn_ss.at[0, h])
        arrived(mx_l.at[h], xn_ss.at[1, h])
        arrived(pb_r.at[h], pn_ss.at[0, h])
        arrived(pb_l.at[h], pn_ss.at[1, h])
    for k in range(1, ny):
        arrived(ysend.at[0], y_ss.at[k])
    for k in range(3):
        arrived(sq_send.at[k], sq_ss.at[k])

    @pl.loop(1, nz)
    def _(k):
        owner = lax.rem(s + k, nz)
        arrived(zm_send.at[0], zm_ss.at[owner])
        arrived(zt_send.at[0], zt_ss.at[owner])

    for k in range(blocks):
        for h in range(1, hops + 1):
            if h < hops:
                arrived(ring.at[0, k], ring_ss.at[0, k, h])
                arrived(ring.at[0, k], ring_ss.at[1, k, h])
            else:

                @pl.when(even)
                def _():
                    arrived(ring.at[0, k], ring_ss.at[0, k, h])

                @pl.when(jnp.logical_not(even))
                def _():
                    arrived(ring.at[0, k], ring_ss.at[1, k, h])


def body(
    nz,
    ny,
    conv_x,
    gate_z,
    step,
    decay_rate,
    state_in,
    state_out,
    skip,
    out_weight,
    residual,
    norm_gain,
    expert_ids,
    expert_weights,
):
    tokens, channels = conv_x.shape
    entries = state_in.shape[1]
    features = expert_weights.shape[2]
    doubled = expert_weights.shape[-1]
    gated = doubled // 2
    half = tokens // 2
    sources = nz // NX
    tail = max(16, sources * TAIL_SLOTS)
    rows = sources * MAIN_SLOTS + tail
    experts = max(nz // 2, 16)
    hops = ny // 2
    groups = nz // STATE_GROUP
    dma = pltpu.SemaphoreType.DMA
    vmem = pltpu.VMEM
    scratch = [
        vmem(out_weight.shape, BF16),
        vmem((tokens, LANES), BF16),
        vmem((features, doubled), BF16),
        vmem((tokens, channels), F32),
        vmem((tokens, channels), F32),
        vmem((tokens, channels), F32),
        vmem((tokens, channels), F32),
        vmem((STATE_GROUP, entries, channels), BF16),
        vmem((STATE_GROUP, 1, channels), F32),
        vmem((groups, entries, channels), BF16),
        vmem((groups, 1, channels), F32),
        vmem((entries, channels), F32),
        vmem((1, channels), F32),
        vmem((2, ny, half, LANES), BF16),
        vmem((2, ny, half, LANES), BF16),
        vmem((2, ny, half, LANES), BF16),
        vmem((ny, half, LANES), F32),
        vmem((ny, half, LANES), F32),
        vmem((2, ny, half, LANES), F32),
        vmem((2, ny, half, LANES), BF16),
        vmem((2, 2, ny, half, LANES), BF16),
        vmem((ny, tokens, LANES), BF16),
        vmem((ny, tokens, LANES), BF16),
        vmem((experts, MAIN_SLOTS, LANES), BF16),
        vmem((experts, TAIL_SLOTS, LANES), F32),
        vmem((nz, MAIN_SLOTS, LANES), BF16),
        vmem((nz, TAIL_SLOTS, LANES), F32),
        vmem((ny, NX, rows, LANES), BF16),
        vmem((rows, features), BF16),
        vmem((2, rows, gated), BF16),
        vmem((2, rows, gated), BF16),
        vmem((2, rows, gated), BF16),
        vmem((rows, gated), F32),
        vmem((rows, gated), F32),
        vmem((2, rows, gated), F32),
        vmem((2, rows, gated), BF16),
        vmem((2, 2, rows, gated), BF16),
        vmem((NX, 8, rows), F32),
        vmem((NX - 1, 8, rows), F32),
        dma((3,)),
        dma((2, STATE_GROUP)),
        dma((2, STATE_GROUP)),
        dma((2, groups)),
        dma((2, groups)),
        dma((2,)),
        dma((2,)),
        dma((2, 2)),
        dma((2, 2)),
        dma((ny,)),
        dma((ny,)),
        dma((nz,)),
        dma((nz,)),
        dma((nz,)),
        dma((nz,)),
        dma((2, NX, hops + 1)),
        dma((2, NX, hops + 1)),
        dma((2,)),
        dma((2,)),
        dma((2, 2)),
        dma((2, 2)),
        dma((NX - 1,)),
        dma((NX - 1,)),
    ]
    whole = pl.BlockSpec(memory_space=pltpu.VMEM)
    far = pl.BlockSpec(memory_space=pl.ANY)
    out_rows = sources * (MAIN_SLOTS + TAIL_SLOTS)
    hidden = pl.pallas_call(
        functools.partial(kernel, nz, ny),
        out_shape=jax.ShapeDtypeStruct((out_rows, gated), BF16),
        in_specs=[whole] * 9 + [far] * 3,
        out_specs=whole,
        scratch_shapes=scratch,
        compiler_params=pltpu.CompilerParams(collective_id=0, has_side_effects=True),
        name="layer",
    )(
        conv_x,
        gate_z,
        step,
        decay_rate.reshape(channels // LANES, LANES),
        state_in.T,
        state_out.T,
        skip.reshape(channels // LANES, LANES),
        norm_gain.reshape(-1, LANES),
        expert_ids.T,
        out_weight,
        residual,
        expert_weights.reshape(features, doubled),
    )
    return hidden.reshape(1, out_rows, 1, gated)


def solution(mesh):
    in_specs = (
        P("seq", ("exp", "ch")),
        P("seq", ("exp", "ch")),
        P("seq", ("exp", "ch")),
        P(("exp", "ch")),
        P("seq", None),
        P("seq", None),
        P(("exp", "ch")),
        P(("exp", "ch"), None),
        P("seq", None),
        P(),
        P("seq", None),
        P("seq", None, "exp", "ch", None),
    )
    return jax.shard_map(
        functools.partial(body, mesh.shape["seq"], mesh.shape["ch"]),
        mesh=mesh,
        in_specs=in_specs,
        out_specs=P("seq", "exp", None, "ch"),
        check_vma=False,
    )
```

```python
import functools

import jax
import jax.numpy as jnp
from jax import lax
from jax.experimental import pallas as pl
from jax.experimental.pallas import tpu as pltpu
from jax.sharding import PartitionSpec as P

MESH = pl.DeviceIdType.MESH
F32 = jnp.float32
BF16 = jnp.bfloat16
EXACT = lax.Precision.HIGHEST
EPSILON = 1e-05
MAIN_SLOTS = 16
TAIL_SLOTS = 2
LANES = 128
STATE_GROUP = 4
NX = 4
PARTS = 2


def silu(v):
    return v / (1.0 + jnp.exp(-v))


def arrived(ref, sem):
    pltpu.make_async_copy(ref, ref, sem).wait()


def send(src, dst, send_sem, recv_sem, device):
    pltpu.make_async_remote_copy(
        src_ref=src,
        dst_ref=dst,
        send_sem=send_sem,
        recv_sem=recv_sem,
        device_id=device,
        device_id_type=MESH,
    ).start()


def kernel(
    nz,
    ny,
    conv_ref,
    gate_ref,
    step_ref,
    rate_ref,
    b_ref,
    c_ref,
    skip_ref,
    gain_ref,
    ids_ref,
    wout_hbm,
    resid_hbm,
    wexp_hbm,
    out_ref,
    wout,
    resid,
    wexp,
    e_ref,
    d_ref,
    y_ref,
    p_ref,
    s1h,
    s1a,
    s2h,
    s2a,
    inc_h,
    pick_main,
    pick_tail,
    arrange,
    mx_opp,
    mx_r,
    mx_l,
    mx_rc,
    mx_lc,
    mx_own,
    xo_recv,
    xn_recv,
    ysend,
    yrecv,
    zm_send,
    zt_send,
    zm_recv,
    zt_recv,
    ring,
    lhs,
    squares,
    pb_opp,
    pb_r,
    pb_l,
    pb_rc,
    pb_lc,
    pb_own,
    po_recv,
    pn_recv,
    sq_send,
    sq_recv,
    local_sem,
    s1_ss,
    s1_rs,
    s2_ss,
    s2_rs,
    xo_ss,
    xo_rs,
    xn_ss,
    xn_rs,
    y_ss,
    y_rs,
    zm_ss,
    zm_rs,
    zt_ss,
    zt_rs,
    ring_ss,
    ring_rs,
    po_ss,
    po_rs,
    pn_ss,
    pn_rs,
    sq_ss,
    sq_rs,
):
    s = lax.axis_index("seq")
    x = lax.axis_index("exp")
    y = lax.axis_index("ch")
    tokens, channels = conv_ref.shape
    features = ny * LANES
    part_tokens = tokens // PARTS
    quarter = part_tokens // 2
    experts = nz // 2
    wide_experts = max(experts, 16)
    sources = nz // NX
    main = sources * MAIN_SLOTS
    tail = sources * TAIL_SLOTS
    block_rows = lhs.shape[1]
    xr, xl, xo = lax.rem(x + 1, NX), lax.rem(x + 3, NX), lax.rem(x + 2, NX)
    yr, yl = lax.rem(y + 1, ny), lax.rem(y + ny - 1, ny)

    barrier = pltpu.get_barrier_semaphore()

    @pl.loop(1, nz)
    def _(k):
        pl.semaphore_signal(
            barrier, inc=1, device_id={"seq": lax.rem(s + k, nz)}, device_id_type=MESH
        )

    for k in range(1, NX):
        pl.semaphore_signal(
            barrier, inc=1, device_id={"exp": lax.rem(x + k, NX)}, device_id_type=MESH
        )
    for k in range(1, ny):
        pl.semaphore_signal(
            barrier, inc=1, device_id={"ch": lax.rem(y + k, ny)}, device_id_type=MESH
        )

    share = pl.multiple_of((x * ny + y) * LANES, LANES)
    copy_wout = pltpu.make_async_copy(wout_hbm, wout, local_sem.at[0])
    copy_resid = pltpu.make_async_copy(
        resid_hbm.at[:, pl.ds(share, LANES)], resid, local_sem.at[1]
    )
    copy_wexp = pltpu.make_async_copy(wexp_hbm, wexp, local_sem.at[2])
    copy_wout.start()
    copy_resid.start()
    copy_wexp.start()

    def wide(ref):
        return jnp.concatenate(
            [ref[k : k + 1, :] for k in range(channels // LANES)], axis=1
        )

    conv = conv_ref[...].astype(F32)
    decay_log = step_ref[...].astype(F32) * wide(rate_ref)
    decay = jnp.exp(-decay_log)
    twice = 2.0 * decay_log
    series = twice * (
        1.0
        - twice
        * (
            1.0 / 2.0
            - twice
            * (
                1.0 / 6.0
                - twice * (1.0 / 24.0 - twice * (1.0 / 120.0 - twice * (1.0 / 720.0)))
            )
        )
    )
    lost = jnp.where(twice < 0.25, series, 1.0 - jnp.exp(-twice))
    e_ref[...] = decay
    d_ref[...] = jnp.sqrt(lost) * conv

    def eight_tokens(i, carry):
        state, product, b_now, c_now = carry
        rows = pl.ds(pl.multiple_of(i * 8, 8), 8)
        e8 = e_ref[rows, :]
        d8 = d_ref[rows, :]
        outs, products = [], []
        for k in range(8):
            e1 = e8[k : k + 1, :]
            state = e1 * state + d8[k : k + 1, :] * b_now[:, k : k + 1]
            product = product * e1
            outs.append(jnp.sum(state * c_now[:, k : k + 1], axis=0, keepdims=True))
            products.append(product)
        y_ref[rows, :] = jnp.concatenate(outs, axis=0)
        p_ref[rows, :] = jnp.concatenate(products, axis=0)
        shift = b_now.shape[1] - 8
        return state, product, pltpu.roll(b_now, shift, 1), pltpu.roll(c_now, shift, 1)

    state, product, _, _ = lax.fori_loop(
        0,
        tokens // 8,
        eight_tokens,
        (
            jnp.zeros((b_ref.shape[0], channels), F32),
            jnp.ones((1, channels), F32),
            b_ref[...],
            c_ref[...],
        ),
    )

    group, place = s // STATE_GROUP, lax.rem(s, STATE_GROUP)
    groups = nz // STATE_GROUP
    s1h[place] = state.astype(BF16)
    s1a[place] = product
    pl.semaphore_wait(barrier, nz - 1 + NX - 1 + ny - 1)
    for k in range(1, STATE_GROUP):
        other = lax.rem(place + k, STATE_GROUP)
        device = {"seq": group * STATE_GROUP + other}
        send(s1h.at[place], s1h.at[place], s1_ss.at[0], s1_rs.at[0], device)
        send(s1a.at[place], s1a.at[place], s1_ss.at[1], s1_rs.at[1], device)
    gates = silu(gate_ref[...].astype(F32))
    within = y_ref[...] + wide(skip_ref) * conv
    arrived(s1h.at[pl.ds(0, STATE_GROUP - 1)], s1_rs.at[0])
    arrived(s1a.at[pl.ds(0, STATE_GROUP - 1)], s1_rs.at[1])
    total_h = jnp.zeros_like(state)
    total_a = jnp.ones_like(product)
    before_h = jnp.zeros_like(state)
    before_a = jnp.ones_like(product)
    for j in range(STATE_GROUP):
        h_j = s1h[j].astype(F32)
        a_j = s1a[j]
        total_h = a_j * total_h + h_j
        total_a = a_j * total_a
        earlier = j < place
        before_h = jnp.where(earlier, a_j * before_h + h_j, before_h)
        before_a = jnp.where(earlier, a_j * before_a, before_a)
    s2h[group] = total_h.astype(BF16)
    s2a[group] = total_a
    for k in range(groups - 1, 0, -1):

        @pl.when(group + k < groups)
        def _():
            device = {"seq": s + k * STATE_GROUP}
            send(s2h.at[group], s2h.at[group], s2_ss.at[0, k], s2_rs.at[0, group], device)
            send(s2a.at[group], s2a.at[group], s2_ss.at[1, k], s2_rs.at[1, group], device)

    names = lax.broadcasted_iota(jnp.int32, (wide_experts, tokens), 0)
    named = (ids_ref[0:1, :] == names) | (ids_ref[1:2, :] == names)
    count = jnp.where(named, 1.0, 0.0)
    before = jnp.where(
        lax.broadcasted_iota(jnp.int32, (tokens, tokens), 0)
        < lax.broadcasted_iota(jnp.int32, (tokens, tokens), 1),
        1.0,
        0.0,
    )
    earlier = jnp.dot(
        count.astype(BF16), before.astype(BF16), preferred_element_type=F32
    )
    slot = jnp.where(named, earlier, -1.0).astype(BF16)

    def picked(slots, first):
        rows = slots * wide_experts
        spread = jnp.where(
            lax.broadcasted_iota(jnp.int32, (rows, wide_experts), 0) // slots
            == lax.broadcasted_iota(jnp.int32, (rows, wide_experts), 1),
            1.0,
            0.0,
        ).astype(BF16)
        per_row = jnp.dot(spread, slot, preferred_element_type=F32)
        wanted = lax.rem(
            lax.broadcasted_iota(jnp.int32, (rows, tokens), 0), slots
        ).astype(F32) + float(first)
        return jnp.where(per_row == wanted, 1.0, 0.0).astype(BF16)

    pick_main[...] = picked(MAIN_SLOTS, 0)
    pick_tail[...] = picked(TAIL_SLOTS, MAIN_SLOTS)
    slots = MAIN_SLOTS + TAIL_SLOTS
    final = lax.broadcasted_iota(jnp.int32, (sources * slots, block_rows), 0)
    place_of = lax.broadcasted_iota(jnp.int32, (sources * slots, block_rows), 1)
    owner_row, slot_row = final // slots, lax.rem(final, slots)
    taken = jnp.where(
        slot_row < MAIN_SLOTS,
        owner_row * MAIN_SLOTS + slot_row,
        main + owner_row * TAIL_SLOTS + slot_row - MAIN_SLOTS,
    )
    arrange[...] = jnp.where(taken == place_of, 1.0, 0.0).astype(BF16)

    inc_h[...] = jnp.zeros_like(state)
    for j in range(groups - 1):

        @pl.when(j < group)
        def _():
            arrived(s2h.at[j], s2_rs.at[0, j])
            arrived(s2a.at[j], s2_rs.at[1, j])
            inc_h[...] = s2a[j] * inc_h[...] + s2h[j].astype(F32)

    incoming = before_a * inc_h[...] + before_h

    carried = lax.dot_general(
        c_ref[...], incoming, (((0,), (0,)), ((), ())), precision=EXACT,
        preferred_element_type=F32,
    )
    mamba = ((within + p_ref[...] * carried) * gates).astype(BF16)
    copy_wout.wait()

    def project(which, store):
        @pl.loop(0, ny // 2)
        def _(n):
            start = pl.multiple_of(which * features + n * 2 * LANES, 2 * LANES)
            part = jnp.dot(
                mamba, wout[:, pl.ds(start, 2 * LANES)], preferred_element_type=F32
            )
            for q in range(PARTS):
                for h in range(2):
                    first = q * part_tokens + h * quarter
                    for j in range(2):
                        store(
                            q,
                            h,
                            2 * n + j,
                            part[first : first + quarter, j * LANES : (j + 1) * LANES],
                        )

    def into_opp(q, h, n, v):
        mx_opp[q, h, n] = v.astype(BF16)

    def into_r(q, h, n, v):
        if h == 0:
            mx_rc[q, n] = v
        else:
            mx_r[q, 1, n] = v.astype(BF16)

    def into_l(q, h, n, v):
        if h == 1:
            mx_lc[q, n] = v
        else:
            mx_l[q, 0, n] = v.astype(BF16)

    def into_own(q, h, n, v):
        mx_own[q, h, n] = v

    to_r, to_l = {"exp": xr}, {"exp": xl}

    def pass_on(side, q, h):
        held, device = (mx_r, to_r) if side == 0 else (mx_l, to_l)
        send(
            held.at[q, h], xn_recv.at[side, q, h], xn_ss.at[side, q, h],
            xn_rs.at[side, q, h], device,
        )

    def add_and_pass_on(q):
        arrived(xo_recv.at[q, 0], xo_rs.at[q, 0])
        mx_r[q, 0] = (mx_rc[q] + xo_recv[q, 0].astype(F32)).astype(BF16)
        pass_on(0, q, 0)
        arrived(xo_recv.at[q, 1], xo_rs.at[q, 1])
        mx_l[q, 1] = (mx_lc[q] + xo_recv[q, 1].astype(F32)).astype(BF16)
        pass_on(1, q, 1)

    project(xo, into_opp)
    for q in range(PARTS):
        send(mx_opp.at[q, 0], xo_recv.at[q, 0], xo_ss.at[q, 0], xo_rs.at[q, 0], to_r)
        send(mx_opp.at[q, 1], xo_recv.at[q, 1], xo_ss.at[q, 1], xo_rs.at[q, 1], to_l)
    project(xr, into_r)
    pass_on(0, 0, 1)
    project(xl, into_l)
    pass_on(1, 0, 0)
    for q in range(PARTS):
        add_and_pass_on(q)
        if q + 1 < PARTS:
            pass_on(0, q + 1, 1)
            pass_on(1, q + 1, 0)
        if q == 0:
            project(x, into_own)

    far_first = sorted(range(1, ny), key=lambda k: -min(k, ny - k))
    for q in range(PARTS):
        for side in range(2):
            for h in (1, 0) if side == 0 else (0, 1):
                arrived(xn_recv.at[side, q, h], xn_rs.at[side, q, h])
        for n in range(ny):
            for h in range(2):
                ysend[q, n, h * quarter : (h + 1) * quarter, :] = (
                    mx_own[q, h, n]
                    + xn_recv[0, q, h, n].astype(F32)
                    + xn_recv[1, q, h, n].astype(F32)
                ).astype(BF16)
        for k in far_first:
            other = lax.rem(y + k, ny)
            send(
                ysend.at[q, other], yrecv.at[q, y], y_ss.at[q], y_rs.at[q],
                {"ch": other},
            )
        yrecv[q, y] = ysend[q, y]
    copy_resid.wait()
    streams = []
    for q in range(PARTS):
        arrived(yrecv.at[q, pl.ds(0, ny - 1)], y_rs.at[q])
        stream = resid[q * part_tokens : (q + 1) * part_tokens, :].astype(F32)
        for n in range(ny):
            stream = stream + yrecv[q, n].astype(F32)
        streams.append(stream)
    rows_of = jnp.concatenate(streams, axis=0).astype(BF16)

    main_rows = jnp.dot(pick_main[...], rows_of, preferred_element_type=F32).astype(BF16)
    tail_rows = jnp.dot(pick_tail[...], rows_of, preferred_element_type=F32)
    zm_send[...] = main_rows.reshape(wide_experts, MAIN_SLOTS, LANES)
    zt_send[...] = tail_rows.reshape(wide_experts, TAIL_SLOTS, LANES)

    def dispatch(owner):
        expert = lax.rem(owner, experts)
        device = {"seq": owner}
        send(zm_send.at[expert], zm_recv.at[s], zm_ss, zm_rs.at[s // sources], device)
        send(zt_send.at[expert], zt_recv.at[s], zt_ss, zt_rs.at[s // sources], device)

    dispatch(lax.rem(s + nz // 2, nz))

    @pl.loop(1, nz // 2)
    def _(k):
        far = nz // 2 - k
        dispatch(lax.rem(s + far, nz))
        dispatch(lax.rem(s + nz - far, nz))

    mine = lax.rem(s, experts)
    zm_recv[s] = zm_send[mine]
    zt_recv[s] = zt_send[mine]

    blocks = NX
    order = [xo, xr, xl, x]
    hops = ny // 2
    even = lax.rem(s, 2) == 0

    def fill(k):
        first = order[k] * sources

        def all_of(number):
            arrived(zm_recv.at[pl.ds(0, number)], zm_rs.at[order[k]])
            arrived(zt_recv.at[pl.ds(0, number)], zt_rs.at[order[k]])

        @pl.when(s // sources == order[k])
        def _():
            all_of(sources - 1)

        @pl.when(s // sources != order[k])
        def _():
            all_of(sources)

        ring[y, k, 0:main, :] = zm_recv[pl.ds(first, sources)].reshape(main, LANES)
        rest = zt_recv[pl.ds(first, sources)].reshape(tail, LANES)
        if tail < 16:
            rest = jnp.concatenate([rest, jnp.zeros((16 - tail, LANES), F32)], axis=0)
        ring[y, k, main:, :] = rest.astype(BF16)

    def hop_right(k, h, first_part):
        held = lax.rem(y + ny - h + 1, ny)
        got = lax.rem(y + ny - h, ny)
        if first_part:
            send(
                ring.at[held, k], ring.at[held, k], ring_ss, ring_rs.at[0, k, h - 1],
                {"ch": yr},
            )
        else:
            arrived(ring.at[got, k], ring_rs.at[0, k, h - 1])

    def hop_left(k, h, first_part):
        held = lax.rem(y + h - 1, ny)
        got = lax.rem(y + h, ny)
        if first_part:
            send(
                ring.at[held, k], ring.at[held, k], ring_ss, ring_rs.at[1, k, h - 1],
                {"ch": yl},
            )
        else:
            arrived(ring.at[got, k], ring_rs.at[1, k, h - 1])

    def hop(k, h, first_part):
        if h < hops:
            hop_right(k, h, first_part)
            hop_left(k, h, first_part)
        else:

            @pl.when(even)
            def _():
                hop_right(k, h, first_part)

            @pl.when(jnp.logical_not(even))
            def _():
                hop_left(k, h, first_part)

    gated = pb_own.shape[-1]
    width = 256

    def prepare(k, n, first):
        v = ring[n, k].astype(F32)
        squares[k] = v * v if first else squares[k] + v * v
        at = pl.ds(pl.multiple_of(n * LANES, LANES), LANES)
        lhs[k, :, at] = (v * gain_ref[pl.ds(x * ny + n, 1), :]).astype(BF16)

    def expert_half(k, h, store):
        @pl.loop(0, gated // width)
        def _(n):
            start = pl.multiple_of(n * width, width)
            column = pl.multiple_of(h * gated + n * width, width)
            part = jnp.dot(
                lhs[k], wexp[:, pl.ds(column, width)], preferred_element_type=F32
            )
            store(h, pl.ds(start, width), part)

    def square_sums(k):
        sq_send[k] = lax.dot_general(
            jnp.ones((8, LANES), F32), squares[k], (((1,), (1,)), ((), ())),
            precision=EXACT, preferred_element_type=F32,
        )

    def keep_opp(h, at, v):
        pb_opp[h, :, at] = v.astype(BF16)

    def keep_r(h, at, v):
        if h == 0:
            pb_rc[:, at] = v
        else:
            pb_r[1, :, at] = v.astype(BF16)

    def keep_l(h, at, v):
        if h == 1:
            pb_lc[:, at] = v
        else:
            pb_l[0, :, at] = v.astype(BF16)

    def keep_own(h, at, v):
        pb_own[h, :, at] = v

    def all_left():
        arrived(s1h.at[pl.ds(0, STATE_GROUP - 1)], s1_ss.at[0])
        arrived(s1a.at[pl.ds(0, STATE_GROUP - 1)], s1_ss.at[1])
        for k in range(1, groups):

            @pl.when(group + k < groups)
            def _():
                arrived(s2h.at[0], s2_ss.at[0, k])
                arrived(s2a.at[0], s2_ss.at[1, k])

        for h in range(2):
            for q in range(PARTS):
                arrived(mx_opp.at[q, h], xo_ss.at[q, h])
                arrived(mx_r.at[q, h], xn_ss.at[0, q, h])
                arrived(mx_l.at[q, h], xn_ss.at[1, q, h])
            arrived(pb_opp.at[h], po_ss.at[h])
        arrived(pb_r.at[1], pn_ss.at[0, 1])
        arrived(pb_l.at[0], pn_ss.at[1, 0])
        for q in range(PARTS):
            arrived(ysend.at[q, pl.ds(0, ny - 1)], y_ss.at[q])
        for k in range(3):
            arrived(sq_send.at[k], sq_ss.at[k])

        arrived(zm_recv.at[pl.ds(0, nz - 1)], zm_ss)
        arrived(zt_recv.at[pl.ds(0, nz - 1)], zt_ss)
        arrived(ring.at[pl.ds(0, ny - 1)], ring_ss)

    def exchange(k, h):
        if h == 1:
            fill(k)
        else:
            hop(k, h - 1, False)
        if h <= hops:
            hop(k, h, True)
        if h == 1:
            prepare(k, y, True)
        else:
            prepare(k, lax.rem(y + h - 1, ny), False)
            if h <= hops:
                prepare(k, lax.rem(y + ny - h + 1, ny), False)

    def opposite_block():
        exchange(0, hops + 1)
        copy_wexp.wait()
        for turn in range(2):
            h = jnp.where(even, turn, 1 - turn)
            expert_half(0, h, keep_opp)
            device = {"exp": jnp.where(h == 0, xr, xl)}
            send(pb_opp.at[h], po_recv.at[h], po_ss.at[h], po_rs.at[h], device)

    at_turn = ((3, 6, 9, 12), (4, 7.5, 13, 16), (5, 10, 14, 17), (7, 11, 15, 18))
    turns = sorted(
        (at_turn[k][h - 1], k, h) for k in range(blocks) for h in range(1, hops + 1)
    )
    first_done = max(i for i, (_, k, _) in enumerate(turns) if k == 0)
    for i, (_, k, h) in enumerate(turns):
        exchange(k, h)
        if i == min(first_done + 3, len(turns) - 1):
            opposite_block()
    exchange(1, hops + 1)
    expert_half(1, 1, keep_r)
    send(pb_r.at[1], pn_recv.at[0, 1], pn_ss.at[0, 1], pn_rs.at[0, 1], to_r)
    exchange(2, hops + 1)
    expert_half(2, 0, keep_l)
    send(pb_l.at[0], pn_recv.at[1, 0], pn_ss.at[1, 0], pn_rs.at[1, 0], to_l)
    for k, device in enumerate(({"exp": xo}, to_r, to_l)):
        square_sums(k)
        send(sq_send.at[k], sq_recv.at[k], sq_ss.at[k], sq_rs.at[k], device)
    expert_half(1, 0, keep_r)
    expert_half(2, 1, keep_l)
    exchange(3, hops + 1)
    square_sums(3)
    for h in range(2):
        expert_half(3, h, keep_own)
    arrived(po_recv.at[0], po_rs.at[0])
    pb_r[0] = (pb_rc[...] + po_recv[0].astype(F32)).astype(BF16)
    send(pb_r.at[0], pn_recv.at[0, 0], pn_ss.at[0, 0], pn_rs.at[0, 0], to_r)
    arrived(po_recv.at[1], po_rs.at[1])
    pb_l[1] = (pb_lc[...] + po_recv[1].astype(F32)).astype(BF16)
    send(pb_l.at[1], pn_recv.at[1, 1], pn_ss.at[1, 1], pn_rs.at[1, 1], to_l)

    all_left()
    for k in range(3):
        arrived(sq_recv.at[k], sq_rs.at[k])
    sums = sq_send[3] + sq_recv[0] + sq_recv[1] + sq_recv[2]
    inverse = lax.rsqrt(sums / (NX * features) + EPSILON)
    scale = lax.dot_general(
        inverse, jnp.full((8, LANES), 0.125, F32), (((0,), (0,)), ((), ())),
        precision=EXACT, preferred_element_type=F32,
    )
    scale = jnp.concatenate([scale] * (width // LANES), axis=1)
    arrived(pn_recv.at[0, 1], pn_rs.at[0, 1])
    pb_own[1] = pb_own[1] + pn_recv[0, 1].astype(F32)
    arrived(pn_recv.at[1, 0], pn_rs.at[1, 0])
    pb_own[0] = pb_own[0] + pn_recv[1, 0].astype(F32)
    arrived(pn_recv.at[0, 0], pn_rs.at[0, 0])
    arrived(pn_recv.at[1, 1], pn_rs.at[1, 1])

    @pl.loop(0, gated // width)
    def _(n):
        at = pl.ds(pl.multiple_of(n * width, width), width)
        gate_part = scale * (pb_own[0, :, at] + pn_recv[0, 0, :, at].astype(F32))
        up_part = scale * (pb_own[1, :, at] + pn_recv[1, 1, :, at].astype(F32))
        hidden = (silu(gate_part) * up_part).astype(BF16)
        out_ref[:, at] = jnp.dot(
            arrange[...], hidden, preferred_element_type=F32
        ).astype(BF16)

    arrived(pb_r.at[0], pn_ss.at[0, 0])
    arrived(pb_l.at[1], pn_ss.at[1, 1])


def body(
    nz,
    ny,
    conv_x,
    gate_z,
    step,
    decay_rate,
    state_in,
    state_out,
    skip,
    out_weight,
    residual,
    norm_gain,
    expert_ids,
    expert_weights,
):
    tokens, channels = conv_x.shape
    entries = state_in.shape[1]
    features = expert_weights.shape[2]
    doubled = expert_weights.shape[-1]
    gated = doubled // 2
    part_tokens = tokens // PARTS
    quarter = part_tokens // 2
    sources = nz // NX
    tail = max(16, sources * TAIL_SLOTS)
    rows = sources * MAIN_SLOTS + tail
    experts = max(nz // 2, 16)
    hops = ny // 2
    groups = nz // STATE_GROUP
    dma = pltpu.SemaphoreType.DMA
    vmem = pltpu.VMEM
    scratch = [
        vmem(out_weight.shape, BF16),
        vmem((tokens, LANES), BF16),
        vmem((features, doubled), BF16),
        vmem((tokens, channels), F32),
        vmem((tokens, channels), F32),
        vmem((tokens, channels), F32),
        vmem((tokens, channels), F32),
        vmem((STATE_GROUP, entries, channels), BF16),
        vmem((STATE_GROUP, 1, channels), F32),
        vmem((groups, entries, channels), BF16),
        vmem((groups, 1, channels), F32),
        vmem((entries, channels), F32),
        vmem((MAIN_SLOTS * experts, tokens), BF16),
        vmem((TAIL_SLOTS * experts, tokens), BF16),
        vmem((sources * (MAIN_SLOTS + TAIL_SLOTS), rows), BF16),
        vmem((PARTS, 2, ny, quarter, LANES), BF16),
        vmem((PARTS, 2, ny, quarter, LANES), BF16),
        vmem((PARTS, 2, ny, quarter, LANES), BF16),
        vmem((PARTS, ny, quarter, LANES), F32),
        vmem((PARTS, ny, quarter, LANES), F32),
        vmem((PARTS, 2, ny, quarter, LANES), F32),
        vmem((PARTS, 2, ny, quarter, LANES), BF16),
        vmem((2, PARTS, 2, ny, quarter, LANES), BF16),
        vmem((PARTS, ny, part_tokens, LANES), BF16),
        vmem((PARTS, ny, part_tokens, LANES), BF16),
        vmem((experts, MAIN_SLOTS, LANES), BF16),
        vmem((experts, TAIL_SLOTS, LANES), F32),
        vmem((nz, MAIN_SLOTS, LANES), BF16),
        vmem((nz, TAIL_SLOTS, LANES), F32),
        vmem((ny, NX, rows, LANES), BF16),
        vmem((NX, rows, features), BF16),
        vmem((NX, rows, LANES), F32),
        vmem((2, rows, gated), BF16),
        vmem((2, rows, gated), BF16),
        vmem((2, rows, gated), BF16),
        vmem((rows, gated), F32),
        vmem((rows, gated), F32),
        vmem((2, rows, gated), F32),
        vmem((2, rows, gated), BF16),
        vmem((2, 2, rows, gated), BF16),
        vmem((NX, 8, rows), F32),
        vmem((NX - 1, 8, rows), F32),
        dma((3,)),
        dma((2,)),
        dma((2,)),
        dma((2, groups)),
        dma((2, groups)),
        dma((PARTS, 2)),
        dma((PARTS, 2)),
        dma((2, PARTS, 2)),
        dma((2, PARTS, 2)),
        dma((PARTS,)),
        dma((PARTS,)),
        dma,
        dma((NX,)),
        dma,
        dma((NX,)),
        dma,
        dma((2, NX, hops)),
        dma((2,)),
        dma((2,)),
        dma((2, 2)),
        dma((2, 2)),
        dma((NX - 1,)),
        dma((NX - 1,)),
    ]
    whole = pl.BlockSpec(memory_space=pltpu.VMEM)
    far = pl.BlockSpec(memory_space=pl.ANY)
    out_rows = sources * (MAIN_SLOTS + TAIL_SLOTS)
    hidden = pl.pallas_call(
        functools.partial(kernel, nz, ny),
        out_shape=pltpu.VMEM((out_rows, gated), BF16),
        in_specs=[whole] * 9 + [far] * 3,
        out_specs=whole,
        scratch_shapes=scratch,
        compiler_params=pltpu.CompilerParams(collective_id=0, has_side_effects=True),
        name="layer",
    )(
        conv_x,
        gate_z,
        step,
        decay_rate.reshape(channels // LANES, LANES),
        state_in.T,
        state_out.T,
        skip.reshape(channels // LANES, LANES),
        norm_gain.reshape(-1, LANES),
        expert_ids.T,
        out_weight,
        residual,
        expert_weights.reshape(features, doubled),
    )
    return hidden.reshape(1, out_rows, 1, gated)


def solution(mesh):
    in_specs = (
        P("seq", ("exp", "ch")),
        P("seq", ("exp", "ch")),
        P("seq", ("exp", "ch")),
        P(("exp", "ch")),
        P("seq", None),
        P("seq", None),
        P(("exp", "ch")),
        P(("exp", "ch"), None),
        P("seq", None),
        P(),
        P("seq", None),
        P("seq", None, "exp", "ch", None),
    )
    return jax.shard_map(
        functools.partial(body, mesh.shape["seq"], mesh.shape["ch"]),
        mesh=mesh,
        in_specs=in_specs,
        out_specs=P("seq", "exp", None, "ch"),
        check_vma=False,
    )
```

```python
import functools

import jax
import jax.numpy as jnp
from jax import lax
from jax.experimental import pallas as pl
from jax.experimental.pallas import tpu as pltpu
from jax.sharding import PartitionSpec as P

MESH = pl.DeviceIdType.MESH
F32 = jnp.float32
BF16 = jnp.bfloat16
EXACT = lax.Precision.HIGHEST
EPSILON = 1e-05
MAIN_SLOTS = 16
TAIL_SLOTS = 2
LANES = 128
STATE_GROUP = 4
NX = 4
PARTS = 4


def silu(v):
    return v / (1.0 + jnp.exp(-v))


def arrived(ref, sem):
    pltpu.make_async_copy(ref, ref, sem).wait()


def send(src, dst, send_sem, recv_sem, device):
    pltpu.make_async_remote_copy(
        src_ref=src,
        dst_ref=dst,
        send_sem=send_sem,
        recv_sem=recv_sem,
        device_id=device,
        device_id_type=MESH,
    ).start()


def kernel(
    nz,
    ny,
    conv_hbm,
    gate_hbm,
    step_hbm,
    rate_hbm,
    b_hbm,
    c_hbm,
    skip_hbm,
    gain_hbm,
    ids_hbm,
    wout_hbm,
    resid_hbm,
    wexp_hbm,
    out_ref,
    conv_ref,
    gate_ref,
    step_ref,
    rate_ref,
    b_ref,
    c_ref,
    skip_ref,
    gain_ref,
    ids_ref,
    wout,
    resid,
    wexp,
    e_ref,
    d_ref,
    y_ref,
    p_ref,
    s1h,
    s1a,
    s2h,
    s2a,
    inc_h,
    pick_main,
    pick_tail,
    arrange,
    mx_opp,
    mx_r,
    mx_l,
    mx_rc,
    mx_lc,
    mx_own,
    xo_recv,
    xn_recv,
    ysend,
    yrecv,
    zm_send,
    zt_send,
    zm_recv,
    zt_recv,
    ring,
    lhs,
    squares,
    pb_opp,
    pb_r,
    pb_l,
    pb_rc,
    pb_lc,
    pb_own,
    po_recv,
    pn_recv,
    sq_send,
    sq_recv,
    local_sem,
    s1_ss,
    s1_rs,
    s2_ss,
    s2_rs,
    xo_ss,
    xo_rs,
    xn_ss,
    xn_rs,
    y_ss,
    y_rs,
    zm_ss,
    zm_rs,
    zt_ss,
    zt_rs,
    ring_ss,
    ring_rs,
    po_ss,
    po_rs,
    pn_ss,
    pn_rs,
    sq_ss,
    sq_rs,
):
    s = lax.axis_index("seq")
    x = lax.axis_index("exp")
    y = lax.axis_index("ch")
    tokens, channels = conv_hbm.shape
    features = ny * LANES
    part_tokens = tokens // PARTS
    quarter = part_tokens // 2
    experts = nz // 2
    wide_experts = max(experts, 16)
    sources = nz // NX
    main = sources * MAIN_SLOTS
    tail = sources * TAIL_SLOTS
    block_rows = lhs.shape[1]
    xr, xl, xo = lax.rem(x + 1, NX), lax.rem(x + 3, NX), lax.rem(x + 2, NX)
    yr, yl = lax.rem(y + 1, ny), lax.rem(y + ny - 1, ny)

    share = pl.multiple_of((x * ny + y) * LANES, LANES)
    taken_in = [
        pltpu.make_async_copy(source, target, local_sem.at[k])
        for k, (source, target) in enumerate(
            (
                (step_hbm, step_ref),
                (rate_hbm, rate_ref),
                (conv_hbm, conv_ref),
                (b_hbm, b_ref),
                (c_hbm, c_ref),
                (gate_hbm, gate_ref),
                (skip_hbm, skip_ref),
                (ids_hbm, ids_ref),
                (gain_hbm, gain_ref),
                (wout_hbm, wout),
                (resid_hbm.at[:, pl.ds(share, LANES)], resid),
                (wexp_hbm, wexp),
            )
        )
    ]
    copy_wout, copy_resid, copy_wexp = taken_in[9:]
    for copy in taken_in[:5]:
        copy.start()

    barrier = pltpu.get_barrier_semaphore()

    @pl.loop(1, nz)
    def _(k):
        pl.semaphore_signal(
            barrier, inc=1, device_id={"seq": lax.rem(s + k, nz)}, device_id_type=MESH
        )

    for k in range(1, NX):
        pl.semaphore_signal(
            barrier, inc=1, device_id={"exp": lax.rem(x + k, NX)}, device_id_type=MESH
        )
    for k in range(1, ny):
        pl.semaphore_signal(
            barrier, inc=1, device_id={"ch": lax.rem(y + k, ny)}, device_id_type=MESH
        )

    for copy in taken_in[5:]:
        copy.start()
    for copy in taken_in[:5]:
        copy.wait()

    def wide(ref):
        return jnp.concatenate(
            [ref[k : k + 1, :] for k in range(channels // LANES)], axis=1
        )

    conv = conv_ref[...].astype(F32)
    decay_log = step_ref[...].astype(F32) * wide(rate_ref)
    decay = jnp.exp(-decay_log)
    twice = 2.0 * decay_log
    series = twice * (
        1.0
        - twice
        * (
            1.0 / 2.0
            - twice
            * (
                1.0 / 6.0
                - twice * (1.0 / 24.0 - twice * (1.0 / 120.0 - twice * (1.0 / 720.0)))
            )
        )
    )
    lost = jnp.where(twice < 0.25, series, 1.0 - jnp.exp(-twice))
    e_ref[...] = decay
    d_ref[...] = jnp.sqrt(lost) * conv

    def eight_tokens(i, carry):
        state, product, b_now, c_now = carry
        rows = pl.ds(pl.multiple_of(i * 8, 8), 8)
        e8 = e_ref[rows, :]
        d8 = d_ref[rows, :]
        outs, products = [], []
        for k in range(8):
            e1 = e8[k : k + 1, :]
            state = e1 * state + d8[k : k + 1, :] * b_now[:, k : k + 1]
            product = product * e1
            outs.append(jnp.sum(state * c_now[:, k : k + 1], axis=0, keepdims=True))
            products.append(product)
        y_ref[rows, :] = jnp.concatenate(outs, axis=0)
        p_ref[rows, :] = jnp.concatenate(products, axis=0)
        shift = b_now.shape[1] - 8
        return state, product, pltpu.roll(b_now, shift, 1), pltpu.roll(c_now, shift, 1)

    state, product, _, _ = lax.fori_loop(
        0,
        tokens // 8,
        eight_tokens,
        (
            jnp.zeros((b_ref.shape[0], channels), F32),
            jnp.ones((1, channels), F32),
            b_ref[...],
            c_ref[...],
        ),
    )

    group, place = s // STATE_GROUP, lax.rem(s, STATE_GROUP)
    groups = nz // STATE_GROUP
    s1h[place] = state.astype(BF16)
    s1a[place] = product
    pl.semaphore_wait(barrier, nz - 1 + NX - 1 + ny - 1)
    for k in range(1, STATE_GROUP):
        other = lax.rem(place + k, STATE_GROUP)
        device = {"seq": group * STATE_GROUP + other}
        send(s1h.at[place], s1h.at[place], s1_ss.at[0], s1_rs.at[0], device)
        send(s1a.at[place], s1a.at[place], s1_ss.at[1], s1_rs.at[1], device)
    for copy in taken_in[5:9]:
        copy.wait()
    gates = silu(gate_ref[...].astype(F32))
    within = y_ref[...] + wide(skip_ref) * conv
    arrived(s1h.at[pl.ds(0, STATE_GROUP - 1)], s1_rs.at[0])
    arrived(s1a.at[pl.ds(0, STATE_GROUP - 1)], s1_rs.at[1])
    total_h = jnp.zeros_like(state)
    total_a = jnp.ones_like(product)
    before_h = jnp.zeros_like(state)
    before_a = jnp.ones_like(product)
    for j in range(STATE_GROUP):
        h_j = s1h[j].astype(F32)
        a_j = s1a[j]
        total_h = a_j * total_h + h_j
        total_a = a_j * total_a
        earlier = j < place
        before_h = jnp.where(earlier, a_j * before_h + h_j, before_h)
        before_a = jnp.where(earlier, a_j * before_a, before_a)
    s2h[group] = total_h.astype(BF16)
    s2a[group] = total_a
    for k in range(groups - 1, 0, -1):

        @pl.when(group + k < groups)
        def _():
            device = {"seq": s + k * STATE_GROUP}
            send(s2h.at[group], s2h.at[group], s2_ss.at[0], s2_rs.at[0], device)
            send(s2a.at[group], s2a.at[group], s2_ss.at[1], s2_rs.at[1], device)

    names = lax.broadcasted_iota(jnp.int32, (wide_experts, tokens), 0)
    named = (ids_ref[0:1, :] == names) | (ids_ref[1:2, :] == names)
    count = jnp.where(named, 1.0, 0.0)
    before = jnp.where(
        lax.broadcasted_iota(jnp.int32, (tokens, tokens), 0)
        < lax.broadcasted_iota(jnp.int32, (tokens, tokens), 1),
        1.0,
        0.0,
    )
    earlier = jnp.dot(
        count.astype(BF16), before.astype(BF16), preferred_element_type=F32
    )
    slot = jnp.where(named, earlier, -1.0).astype(BF16)

    def picked(slots, first):
        rows = slots * wide_experts
        spread = jnp.where(
            lax.broadcasted_iota(jnp.int32, (rows, wide_experts), 0) // slots
            == lax.broadcasted_iota(jnp.int32, (rows, wide_experts), 1),
            1.0,
            0.0,
        ).astype(BF16)
        per_row = jnp.dot(spread, slot, preferred_element_type=F32)
        wanted = lax.rem(
            lax.broadcasted_iota(jnp.int32, (rows, tokens), 0), slots
        ).astype(F32) + float(first)
        return jnp.where(per_row == wanted, 1.0, 0.0).astype(BF16)

    pick_main[...] = picked(MAIN_SLOTS, 0)
    pick_tail[...] = picked(TAIL_SLOTS, MAIN_SLOTS)
    slots = MAIN_SLOTS + TAIL_SLOTS
    final = lax.broadcasted_iota(jnp.int32, (sources * slots, block_rows), 0)
    place_of = lax.broadcasted_iota(jnp.int32, (sources * slots, block_rows), 1)
    owner_row, slot_row = final // slots, lax.rem(final, slots)
    taken = jnp.where(
        slot_row < MAIN_SLOTS,
        owner_row * MAIN_SLOTS + slot_row,
        main + owner_row * TAIL_SLOTS + slot_row - MAIN_SLOTS,
    )
    arrange[...] = jnp.where(taken == place_of, 1.0, 0.0).astype(BF16)

    inc_h[...] = jnp.zeros_like(state)
    for j in range(1, groups):

        @pl.when(j == group)
        def _():
            arrived(s2h.at[pl.ds(0, j)], s2_rs.at[0])
            arrived(s2a.at[pl.ds(0, j)], s2_rs.at[1])

    for j in range(groups - 1):

        @pl.when(j < group)
        def _():
            inc_h[...] = s2a[j] * inc_h[...] + s2h[j].astype(F32)

    incoming = before_a * inc_h[...] + before_h

    carried = lax.dot_general(
        c_ref[...], incoming, (((0,), (0,)), ((), ())), precision=EXACT,
        preferred_element_type=F32,
    )
    mamba = ((within + p_ref[...] * carried) * gates).astype(BF16)
    copy_wout.wait()

    def project(which, store):
        @pl.loop(0, ny // 2)
        def _(n):
            start = pl.multiple_of(which * features + n * 2 * LANES, 2 * LANES)
            part = jnp.dot(
                mamba, wout[:, pl.ds(start, 2 * LANES)], preferred_element_type=F32
            )
            for q in range(PARTS):
                for h in range(2):
                    first = q * part_tokens + h * quarter
                    for j in range(2):
                        store(
                            q,
                            h,
                            2 * n + j,
                            part[first : first + quarter, j * LANES : (j + 1) * LANES],
                        )

    def into_opp(q, h, n, v):
        mx_opp[q, h, n] = v.astype(BF16)

    def into_r(q, h, n, v):
        if h == 0:
            mx_rc[q, n] = v
        else:
            mx_r[q, 1, n] = v.astype(BF16)

    def into_l(q, h, n, v):
        if h == 1:
            mx_lc[q, n] = v
        else:
            mx_l[q, 0, n] = v.astype(BF16)

    def into_own(q, h, n, v):
        mx_own[q, h, n] = v

    to_r, to_l = {"exp": xr}, {"exp": xl}

    def pass_on(side, q, h):
        held, device = (mx_r, to_r) if side == 0 else (mx_l, to_l)
        send(
            held.at[q, h], xn_recv.at[q, side, h], xn_ss.at[side], xn_rs.at[q], device,
        )

    def add_and_pass_on(q):
        arrived(xo_recv.at[q], xo_rs.at[q])
        mx_r[q, 0] = (mx_rc[q] + xo_recv[q, 0].astype(F32)).astype(BF16)
        pass_on(0, q, 0)
        mx_l[q, 1] = (mx_lc[q] + xo_recv[q, 1].astype(F32)).astype(BF16)
        pass_on(1, q, 1)

    project(xo, into_opp)
    for q in range(PARTS):
        send(mx_opp.at[q, 0], xo_recv.at[q, 0], xo_ss, xo_rs.at[q], to_r)
        send(mx_opp.at[q, 1], xo_recv.at[q, 1], xo_ss, xo_rs.at[q], to_l)
    project(xr, into_r)
    pass_on(0, 0, 1)
    project(xl, into_l)
    pass_on(1, 0, 0)
    for q in range(PARTS):
        add_and_pass_on(q)
        if q + 1 < PARTS:
            pass_on(0, q + 1, 1)
            pass_on(1, q + 1, 0)
        if q == 0:
            project(x, into_own)

    far_first = sorted(range(1, ny), key=lambda k: -min(k, ny - k))
    for q in range(PARTS):
        arrived(xn_recv.at[q], xn_rs.at[q])
        for n in range(ny):
            for h in range(2):
                ysend[q, n, h * quarter : (h + 1) * quarter, :] = (
                    mx_own[q, h, n]
                    + xn_recv[q, 0, h, n].astype(F32)
                    + xn_recv[q, 1, h, n].astype(F32)
                ).astype(BF16)
        for k in far_first:
            other = lax.rem(y + k, ny)
            send(
                ysend.at[q, other], yrecv.at[q, y], y_ss, y_rs.at[q],
                {"ch": other},
            )
        yrecv[q, y] = ysend[q, y]
    copy_resid.wait()
    streams = []
    for q in range(PARTS):
        arrived(yrecv.at[q, pl.ds(0, ny - 1)], y_rs.at[q])
        stream = resid[q * part_tokens : (q + 1) * part_tokens, :].astype(F32)
        for n in range(ny):
            stream = stream + yrecv[q, n].astype(F32)
        streams.append(stream)
    rows_of = jnp.concatenate(streams, axis=0).astype(BF16)

    main_rows = jnp.dot(pick_main[...], rows_of, preferred_element_type=F32).astype(BF16)
    tail_rows = jnp.dot(pick_tail[...], rows_of, preferred_element_type=F32)
    zm_send[...] = main_rows.reshape(wide_experts, MAIN_SLOTS, LANES)
    zt_send[...] = tail_rows.reshape(wide_experts, TAIL_SLOTS, LANES)

    def dispatch(owner):
        expert = lax.rem(owner, experts)
        device = {"seq": owner}
        send(zm_send.at[expert], zm_recv.at[s], zm_ss, zm_rs.at[s // sources], device)
        send(zt_send.at[expert], zt_recv.at[s], zt_ss, zt_rs.at[s // sources], device)

    dispatch(lax.rem(s + nz // 2, nz))

    @pl.loop(1, nz // 2)
    def _(k):
        far = nz // 2 - k
        dispatch(lax.rem(s + far, nz))
        dispatch(lax.rem(s + nz - far, nz))

    mine = lax.rem(s, experts)
    zm_recv[s] = zm_send[mine]
    zt_recv[s] = zt_send[mine]

    blocks = NX
    order = [xo, xr, xl, x]
    hops = ny // 2
    even = lax.rem(s, 2) == 0

    def fill(k):
        first = order[k] * sources

        def all_of(number):
            arrived(zm_recv.at[pl.ds(0, number)], zm_rs.at[order[k]])
            arrived(zt_recv.at[pl.ds(0, number)], zt_rs.at[order[k]])

        @pl.when(s // sources == order[k])
        def _():
            all_of(sources - 1)

        @pl.when(s // sources != order[k])
        def _():
            all_of(sources)

        ring[y, k, 0:main, :] = zm_recv[pl.ds(first, sources)].reshape(main, LANES)
        rest = zt_recv[pl.ds(first, sources)].reshape(tail, LANES)
        if tail < 16:
            rest = jnp.concatenate([rest, jnp.zeros((16 - tail, LANES), F32)], axis=0)
        ring[y, k, main:, :] = rest.astype(BF16)

    gated = pb_own.shape[-1]
    width = 256

    def prepare(k, n, first):
        v = ring[n, k].astype(F32)
        squares[k] = v * v if first else squares[k] + v * v
        at = pl.ds(pl.multiple_of(n * LANES, LANES), LANES)
        lhs[k, :, at] = (v * gain_ref[pl.ds(x * ny + n, 1), :]).astype(BF16)

    def expert_half(k, h, store):
        @pl.loop(0, gated // width)
        def _(n):
            start = pl.multiple_of(n * width, width)
            column = pl.multiple_of(h * gated + n * width, width)
            part = jnp.dot(
                lhs[k], wexp[:, pl.ds(column, width)], preferred_element_type=F32
            )
            store(h, pl.ds(start, width), part)

    def square_sums(k):
        sq_send[k] = lax.dot_general(
            jnp.ones((8, LANES), F32), squares[k], (((1,), (1,)), ((), ())),
            precision=EXACT, preferred_element_type=F32,
        )

    def keep_opp(h, at, v):
        pb_opp[h, :, at] = v.astype(BF16)

    def keep_r(h, at, v):
        if h == 0:
            pb_rc[:, at] = v
        else:
            pb_r[1, :, at] = v.astype(BF16)

    def keep_l(h, at, v):
        if h == 1:
            pb_lc[:, at] = v
        else:
            pb_l[0, :, at] = v.astype(BF16)

    def keep_own(h, at, v):
        pb_own[h, :, at] = v

    def all_left():
        arrived(s1h.at[pl.ds(0, STATE_GROUP - 1)], s1_ss.at[0])
        arrived(s1a.at[pl.ds(0, STATE_GROUP - 1)], s1_ss.at[1])
        for k in range(1, groups):

            @pl.when(group + k == groups - 1)
            def _():
                arrived(s2h.at[pl.ds(0, k)], s2_ss.at[0])
                arrived(s2a.at[pl.ds(0, k)], s2_ss.at[1])

        arrived(mx_opp, xo_ss)
        arrived(mx_r, xn_ss.at[0])
        arrived(mx_l, xn_ss.at[1])
        arrived(pb_opp, po_ss)
        arrived(ysend.at[:, pl.ds(0, ny - 1)], y_ss)
        arrived(sq_send.at[pl.ds(0, NX - 1)], sq_ss)

        arrived(zm_recv.at[pl.ds(0, nz - 1)], zm_ss)
        arrived(zt_recv.at[pl.ds(0, nz - 1)], zt_ss)
        arrived(ring.at[pl.ds(0, ny - 1)], ring_ss)

    def near(k):
        return lax.rem(y + ny + k, ny)

    def give(k, chunk, which, target):
        send(
            ring.at[chunk, k], ring.at[chunk, k], ring_ss, ring_rs.at[k, which],
            {"ch": near(target)},
        )

    def first_round(k):
        fill(k)
        if hops == 4:
            give(k, y, 0, 2)
            give(k, y, 1, -2)
            give(k, y, 2, 1)
            give(k, y, 2, -1)
        else:
            for other in far_first:
                give(k, y, 3, other)
        prepare(k, y, True)

    def second_round(k):
        if hops == 4:
            arrived(ring.at[near(-2), k], ring_rs.at[k, 0])

            @pl.when(even)
            def _():
                give(k, near(-2), 3, 2)

            give(k, near(-2), 3, 1)
            arrived(ring.at[near(2), k], ring_rs.at[k, 1])

            @pl.when(jnp.logical_not(even))
            def _():
                give(k, near(2), 3, -2)

            give(k, near(2), 3, -1)
            prepare(k, near(-2), False)
            prepare(k, near(2), False)
            arrived(ring.at[pl.ds(0, 2), k], ring_rs.at[k, 2])
            prepare(k, near(-1), False)
            prepare(k, near(1), False)

    def all_in(k):
        if hops == 4:
            arrived(ring.at[pl.ds(0, 3), k], ring_rs.at[k, 3])
            for other in (3, 4, 5):
                prepare(k, near(other), False)
        else:
            arrived(ring.at[pl.ds(0, ny - 1), k], ring_rs.at[k, 3])
            for other in range(1, ny):
                prepare(k, near(other), False)

    def opposite_half(turn):
        h = jnp.where(even, turn, 1 - turn)
        expert_half(0, h, keep_opp)
        device = {"exp": jnp.where(h == 0, xr, xl)}
        send(pb_opp.at[h], po_recv.at[h], po_ss, po_rs.at[h], device)

    first_round(0)
    first_round(1)
    second_round(0)
    first_round(2)
    second_round(1)
    all_in(0)
    copy_wexp.wait()
    opposite_half(0)
    opposite_half(1)
    second_round(2)
    first_round(3)
    all_in(1)
    expert_half(1, 1, keep_r)
    send(pb_r.at[1], pn_recv.at[0, 0], pn_ss.at[0], pn_rs.at[0], to_r)
    all_in(2)
    expert_half(2, 0, keep_l)
    send(pb_l.at[0], pn_recv.at[0, 1], pn_ss.at[1], pn_rs.at[0], to_l)
    second_round(3)
    for k, device in enumerate(({"exp": xo}, to_r, to_l)):
        square_sums(k)
        send(sq_send.at[k], sq_recv.at[k], sq_ss, sq_rs, device)
    expert_half(1, 0, keep_r)
    expert_half(2, 1, keep_l)
    arrived(po_recv.at[0], po_rs.at[0])
    pb_r[0] = (pb_rc[...] + po_recv[0].astype(F32)).astype(BF16)
    send(pb_r.at[0], pn_recv.at[1, 0], pn_ss.at[0], pn_rs.at[1], to_r)
    arrived(po_recv.at[1], po_rs.at[1])
    pb_l[1] = (pb_lc[...] + po_recv[1].astype(F32)).astype(BF16)
    send(pb_l.at[1], pn_recv.at[1, 1], pn_ss.at[1], pn_rs.at[1], to_l)
    all_in(3)
    square_sums(3)
    for h in range(2):
        expert_half(3, h, keep_own)

    all_left()
    arrived(sq_recv, sq_rs)
    sums = sq_send[3] + sq_recv[0] + sq_recv[1] + sq_recv[2]
    inverse = lax.rsqrt(sums / (NX * features) + EPSILON)
    scale = lax.dot_general(
        inverse, jnp.full((8, LANES), 0.125, F32), (((0,), (0,)), ((), ())),
        precision=EXACT, preferred_element_type=F32,
    )
    scale = jnp.concatenate([scale] * (width // LANES), axis=1)
    arrived(pn_recv.at[0], pn_rs.at[0])
    pb_own[1] = pb_own[1] + pn_recv[0, 0].astype(F32)
    pb_own[0] = pb_own[0] + pn_recv[0, 1].astype(F32)
    arrived(pn_recv.at[1], pn_rs.at[1])

    @pl.loop(0, gated // width)
    def _(n):
        at = pl.ds(pl.multiple_of(n * width, width), width)
        gate_part = scale * (pb_own[0, :, at] + pn_recv[1, 0, :, at].astype(F32))
        up_part = scale * (pb_own[1, :, at] + pn_recv[1, 1, :, at].astype(F32))
        hidden = (silu(gate_part) * up_part).astype(BF16)
        out_ref[:, at] = jnp.dot(
            arrange[...], hidden, preferred_element_type=F32
        ).astype(BF16)

    arrived(pb_r, pn_ss.at[0])
    arrived(pb_l, pn_ss.at[1])


def body(
    nz,
    ny,
    conv_x,
    gate_z,
    step,
    decay_rate,
    state_in,
    state_out,
    skip,
    out_weight,
    residual,
    norm_gain,
    expert_ids,
    expert_weights,
):
    tokens, channels = conv_x.shape
    entries = state_in.shape[1]
    features = expert_weights.shape[2]
    doubled = expert_weights.shape[-1]
    gated = doubled // 2
    part_tokens = tokens // PARTS
    quarter = part_tokens // 2
    sources = nz // NX
    tail = max(16, sources * TAIL_SLOTS)
    rows = sources * MAIN_SLOTS + tail
    experts = max(nz // 2, 16)
    hops = ny // 2
    groups = nz // STATE_GROUP
    dma = pltpu.SemaphoreType.DMA
    vmem = pltpu.VMEM
    scratch = [
        vmem((tokens, channels), BF16),
        vmem((tokens, channels), BF16),
        vmem((tokens, channels), BF16),
        vmem((channels // LANES, LANES), F32),
        vmem((entries, tokens), F32),
        vmem((entries, tokens), F32),
        vmem((channels // LANES, LANES), F32),
        vmem((norm_gain.shape[0] // LANES, LANES), F32),
        vmem((2, tokens), jnp.int32),
        vmem(out_weight.shape, BF16),
        vmem((tokens, LANES), BF16),
        vmem((features, doubled), BF16),
        vmem((tokens, channels), F32),
        vmem((tokens, channels), F32),
        vmem((tokens, channels), F32),
        vmem((tokens, channels), F32),
        vmem((STATE_GROUP, entries, channels), BF16),
        vmem((STATE_GROUP, 1, channels), F32),
        vmem((groups, entries, channels), BF16),
        vmem((groups, 1, channels), F32),
        vmem((entries, channels), F32),
        vmem((MAIN_SLOTS * experts, tokens), BF16),
        vmem((TAIL_SLOTS * experts, tokens), BF16),
        vmem((sources * (MAIN_SLOTS + TAIL_SLOTS), rows), BF16),
        vmem((PARTS, 2, ny, quarter, LANES), BF16),
        vmem((PARTS, 2, ny, quarter, LANES), BF16),
        vmem((PARTS, 2, ny, quarter, LANES), BF16),
        vmem((PARTS, ny, quarter, LANES), F32),
        vmem((PARTS, ny, quarter, LANES), F32),
        vmem((PARTS, 2, ny, quarter, LANES), F32),
        vmem((PARTS, 2, ny, quarter, LANES), BF16),
        vmem((PARTS, 2, 2, ny, quarter, LANES), BF16),
        vmem((PARTS, ny, part_tokens, LANES), BF16),
        vmem((PARTS, ny, part_tokens, LANES), BF16),
        vmem((experts, MAIN_SLOTS, LANES), BF16),
        vmem((experts, TAIL_SLOTS, LANES), F32),
        vmem((nz, MAIN_SLOTS, LANES), BF16),
        vmem((nz, TAIL_SLOTS, LANES), F32),
        vmem((ny, NX, rows, LANES), BF16),
        vmem((NX, rows, features), BF16),
        vmem((NX, rows, LANES), F32),
        vmem((2, rows, gated), BF16),
        vmem((2, rows, gated), BF16),
        vmem((2, rows, gated), BF16),
        vmem((rows, gated), F32),
        vmem((rows, gated), F32),
        vmem((2, rows, gated), F32),
        vmem((2, rows, gated), BF16),
        vmem((2, 2, rows, gated), BF16),
        vmem((NX, 8, rows), F32),
        vmem((NX - 1, 8, rows), F32),
        dma((12,)),
        dma((2,)),
        dma((2,)),
        dma((2,)),
        dma((2,)),
        dma,
        dma((PARTS,)),
        dma((2,)),
        dma((PARTS,)),
        dma,
        dma((PARTS,)),
        dma,
        dma((NX,)),
        dma,
        dma((NX,)),
        dma,
        dma((NX, 4)),
        dma,
        dma((2,)),
        dma((2,)),
        dma((2,)),
        dma,
        dma,
    ]
    whole = pl.BlockSpec(memory_space=pltpu.VMEM)
    far = pl.BlockSpec(memory_space=pl.ANY)
    out_rows = sources * (MAIN_SLOTS + TAIL_SLOTS)
    hidden = pl.pallas_call(
        functools.partial(kernel, nz, ny),
        out_shape=pltpu.VMEM((out_rows, gated), BF16),
        in_specs=[far] * 12,
        out_specs=whole,
        scratch_shapes=scratch,
        compiler_params=pltpu.CompilerParams(collective_id=0, has_side_effects=True),
        name="layer",
    )(
        conv_x,
        gate_z,
        step,
        decay_rate.reshape(channels // LANES, LANES),
        state_in.T,
        state_out.T,
        skip.reshape(channels // LANES, LANES),
        norm_gain.reshape(-1, LANES),
        expert_ids.T,
        out_weight,
        residual,
        expert_weights.reshape(features, doubled),
    )
    return hidden.reshape(1, out_rows, 1, gated)


def solution(mesh):
    in_specs = (
        P("seq", ("exp", "ch")),
        P("seq", ("exp", "ch")),
        P("seq", ("exp", "ch")),
        P(("exp", "ch")),
        P("seq", None),
        P("seq", None),
        P(("exp", "ch")),
        P(("exp", "ch"), None),
        P("seq", None),
        P(),
        P("seq", None),
        P("seq", None, "exp", "ch", None),
    )
    return jax.shard_map(
        functools.partial(body, mesh.shape["seq"], mesh.shape["ch"]),
        mesh=mesh,
        in_specs=in_specs,
        out_specs=P("seq", "exp", None, "ch"),
        check_vma=False,
    )
```

```python
import functools

import jax
import jax.numpy as jnp
from jax import lax
from jax.experimental import pallas as pl
from jax.experimental.pallas import tpu as pltpu
from jax.sharding import PartitionSpec as P

MESH = pl.DeviceIdType.MESH
F32 = jnp.float32
BF16 = jnp.bfloat16
EXACT = lax.Precision.HIGHEST
EPSILON = 1e-05
MAIN_SLOTS = 16
TAIL_SLOTS = 2
LANES = 128
STATE_GROUP = 4
NX = 4
PARTS = 4


def silu(v):
    return v / (1.0 + jnp.exp(-v))


def arrived(ref, sem):
    pltpu.make_async_copy(ref, ref, sem).wait()


def send(src, dst, send_sem, recv_sem, device):
    pltpu.make_async_remote_copy(
        src_ref=src,
        dst_ref=dst,
        send_sem=send_sem,
        recv_sem=recv_sem,
        device_id=device,
        device_id_type=MESH,
    ).start()


def kernel(
    nz,
    ny,
    conv_hbm,
    gate_hbm,
    step_hbm,
    rate_hbm,
    b_hbm,
    c_hbm,
    skip_hbm,
    gain_hbm,
    ids_hbm,
    wout_hbm,
    resid_hbm,
    wexp_hbm,
    out_ref,
    conv_ref,
    gate_ref,
    step_ref,
    rate_ref,
    b_ref,
    c_ref,
    skip_ref,
    gain_ref,
    ids_ref,
    wout,
    resid,
    wexp,
    e_ref,
    d_ref,
    y_ref,
    p_ref,
    s1h,
    s1a,
    s2h,
    s2a,
    inc_h,
    pick_main,
    pick_tail,
    arrange,
    mx_opp,
    mx_r,
    mx_l,
    mx_rc,
    mx_lc,
    mx_own,
    xo_recv,
    xn_recv,
    ysend,
    yrecv,
    zm_send,
    zt_send,
    zm_recv,
    zt_recv,
    ring,
    lhs,
    squares,
    pb_opp,
    pb_r,
    pb_l,
    pb_rc,
    pb_lc,
    pb_own,
    po_recv,
    pn_recv,
    sq_send,
    sq_recv,
    local_sem,
    s1_ss,
    s1_rs,
    s2_ss,
    s2_rs,
    xo_ss,
    xo_rs,
    xn_ss,
    xn_rs,
    y_ss,
    y_rs,
    zm_ss,
    zm_rs,
    zt_ss,
    zt_rs,
    ring_ss,
    ring_rs,
    po_ss,
    po_rs,
    pn_ss,
    pn_rs,
    sq_ss,
    sq_rs,
):
    s = lax.axis_index("seq")
    x = lax.axis_index("exp")
    y = lax.axis_index("ch")
    tokens, channels = conv_hbm.shape
    features = ny * LANES
    part_tokens = tokens // PARTS
    quarter = part_tokens // 2
    experts = nz // 2
    wide_experts = max(experts, 16)
    sources = nz // NX
    main = sources * MAIN_SLOTS
    tail = sources * TAIL_SLOTS
    block_rows = lhs.shape[1]
    xr, xl, xo = lax.rem(x + 1, NX), lax.rem(x + 3, NX), lax.rem(x + 2, NX)
    yr, yl = lax.rem(y + 1, ny), lax.rem(y + ny - 1, ny)

    share = pl.multiple_of((x * ny + y) * LANES, LANES)
    taken_in = [
        pltpu.make_async_copy(source, target, local_sem.at[k])
        for k, (source, target) in enumerate(
            (
                (step_hbm, step_ref),
                (rate_hbm, rate_ref),
                (conv_hbm, conv_ref),
                (b_hbm, b_ref),
                (c_hbm, c_ref),
                (gate_hbm, gate_ref),
                (skip_hbm, skip_ref),
                (ids_hbm, ids_ref),
                (gain_hbm, gain_ref),
                (wout_hbm, wout),
                (resid_hbm.at[:, pl.ds(share, LANES)], resid),
                (wexp_hbm, wexp),
            )
        )
    ]
    copy_wout, copy_resid, copy_wexp = taken_in[9:]
    for copy in taken_in[:5]:
        copy.start()

    barrier = pltpu.get_barrier_semaphore()

    def greet(device):
        pl.semaphore_signal(barrier, inc=1, device_id=device, device_id_type=MESH)

    greet({"seq": lax.rem(s + nz // 2, nz)})

    @pl.loop(1, nz // 2)
    def _(k):
        far = nz // 2 - k
        greet({"seq": lax.rem(s + far, nz)})
        greet({"seq": lax.rem(s + nz - far, nz)})

    for k in range(1, NX):
        greet({"exp": lax.rem(x + k, NX)})
    for k in range(1, ny):
        greet({"ch": lax.rem(y + k, ny)})
    for copy in taken_in[5:]:
        copy.start()
    for copy in taken_in[:5]:
        copy.wait()

    def wide(ref):
        return jnp.concatenate(
            [ref[k : k + 1, :] for k in range(channels // LANES)], axis=1
        )

    conv = conv_ref[...].astype(F32)
    decay_log = step_ref[...].astype(F32) * wide(rate_ref)
    decay = jnp.exp(-decay_log)
    twice = 2.0 * decay_log
    series = twice * (
        1.0
        - twice
        * (
            1.0 / 2.0
            - twice
            * (
                1.0 / 6.0
                - twice * (1.0 / 24.0 - twice * (1.0 / 120.0 - twice * (1.0 / 720.0)))
            )
        )
    )
    lost = jnp.where(twice < 0.25, series, 1.0 - jnp.exp(-twice))
    e_ref[...] = decay
    d_ref[...] = jnp.sqrt(lost) * conv

    def eight_tokens(i, carry):
        state, product, b_now, c_now = carry
        rows = pl.ds(pl.multiple_of(i * 8, 8), 8)
        e8 = e_ref[rows, :]
        d8 = d_ref[rows, :]
        outs, products = [], []
        for k in range(8):
            e1 = e8[k : k + 1, :]
            state = e1 * state + d8[k : k + 1, :] * b_now[:, k : k + 1]
            product = product * e1
            outs.append(jnp.sum(state * c_now[:, k : k + 1], axis=0, keepdims=True))
            products.append(product)
        y_ref[rows, :] = jnp.concatenate(outs, axis=0)
        p_ref[rows, :] = jnp.concatenate(products, axis=0)
        shift = b_now.shape[1] - 8
        return state, product, pltpu.roll(b_now, shift, 1), pltpu.roll(c_now, shift, 1)

    state, product, _, _ = lax.fori_loop(
        0,
        tokens // 8,
        eight_tokens,
        (
            jnp.zeros((b_ref.shape[0], channels), F32),
            jnp.ones((1, channels), F32),
            b_ref[...],
            c_ref[...],
        ),
    )

    group, place = s // STATE_GROUP, lax.rem(s, STATE_GROUP)
    groups = nz // STATE_GROUP
    s1h[place] = state.astype(BF16)
    s1a[place] = product
    pl.semaphore_wait(barrier, nz - 1 + NX - 1 + ny - 1)
    for k in range(1, STATE_GROUP):
        other = lax.rem(place + k, STATE_GROUP)
        device = {"seq": group * STATE_GROUP + other}
        send(s1h.at[place], s1h.at[place], s1_ss.at[0], s1_rs.at[0], device)
        send(s1a.at[place], s1a.at[place], s1_ss.at[1], s1_rs.at[1], device)
    for copy in taken_in[5:9]:
        copy.wait()
    gates = silu(gate_ref[...].astype(F32))
    within = y_ref[...] + wide(skip_ref) * conv
    arrived(s1h.at[pl.ds(0, STATE_GROUP - 1)], s1_rs.at[0])
    arrived(s1a.at[pl.ds(0, STATE_GROUP - 1)], s1_rs.at[1])
    total_h = jnp.zeros_like(state)
    total_a = jnp.ones_like(product)
    before_h = jnp.zeros_like(state)
    before_a = jnp.ones_like(product)
    for j in range(STATE_GROUP):
        h_j = s1h[j].astype(F32)
        a_j = s1a[j]
        total_h = a_j * total_h + h_j
        total_a = a_j * total_a
        earlier = j < place
        before_h = jnp.where(earlier, a_j * before_h + h_j, before_h)
        before_a = jnp.where(earlier, a_j * before_a, before_a)
    s2h[group] = total_h.astype(BF16)
    s2a[group] = total_a
    for k in range(groups - 1, 0, -1):

        @pl.when(group + k < groups)
        def _():
            device = {"seq": s + k * STATE_GROUP}
            send(s2h.at[group], s2h.at[group], s2_ss.at[0], s2_rs.at[0], device)
            send(s2a.at[group], s2a.at[group], s2_ss.at[1], s2_rs.at[1], device)

    names = lax.broadcasted_iota(jnp.int32, (wide_experts, tokens), 0)
    named = (ids_ref[0:1, :] == names) | (ids_ref[1:2, :] == names)
    count = jnp.where(named, 1.0, 0.0)
    before = jnp.where(
        lax.broadcasted_iota(jnp.int32, (tokens, tokens), 0)
        < lax.broadcasted_iota(jnp.int32, (tokens, tokens), 1),
        1.0,
        0.0,
    )
    earlier = jnp.dot(
        count.astype(BF16), before.astype(BF16), preferred_element_type=F32
    )
    slot = jnp.where(named, earlier, -1.0).astype(BF16)

    def picked(slots, first):
        rows = slots * wide_experts
        spread = jnp.where(
            lax.broadcasted_iota(jnp.int32, (rows, wide_experts), 0) // slots
            == lax.broadcasted_iota(jnp.int32, (rows, wide_experts), 1),
            1.0,
            0.0,
        ).astype(BF16)
        per_row = jnp.dot(spread, slot, preferred_element_type=F32)
        wanted = lax.rem(
            lax.broadcasted_iota(jnp.int32, (rows, tokens), 0), slots
        ).astype(F32) + float(first)
        return jnp.where(per_row == wanted, 1.0, 0.0).astype(BF16)

    pick_main[...] = picked(MAIN_SLOTS, 0)
    pick_tail[...] = picked(TAIL_SLOTS, MAIN_SLOTS)
    slots = MAIN_SLOTS + TAIL_SLOTS
    final = lax.broadcasted_iota(jnp.int32, (sources * slots, block_rows), 0)
    place_of = lax.broadcasted_iota(jnp.int32, (sources * slots, block_rows), 1)
    owner_row, slot_row = final // slots, lax.rem(final, slots)
    taken = jnp.where(
        slot_row < MAIN_SLOTS,
        owner_row * MAIN_SLOTS + slot_row,
        main + owner_row * TAIL_SLOTS + slot_row - MAIN_SLOTS,
    )
    arrange[...] = jnp.where(taken == place_of, 1.0, 0.0).astype(BF16)

    inc_h[...] = jnp.zeros_like(state)
    for j in range(1, groups):

        @pl.when(j == group)
        def _():
            arrived(s2h.at[pl.ds(0, j)], s2_rs.at[0])
            arrived(s2a.at[pl.ds(0, j)], s2_rs.at[1])

    for j in range(groups - 1):

        @pl.when(j < group)
        def _():
            inc_h[...] = s2a[j] * inc_h[...] + s2h[j].astype(F32)

    incoming = before_a * inc_h[...] + before_h

    carried = lax.dot_general(
        c_ref[...], incoming, (((0,), (0,)), ((), ())), precision=EXACT,
        preferred_element_type=F32,
    )
    mamba = ((within + p_ref[...] * carried) * gates).astype(BF16)
    copy_wout.wait()

    def project(which, store):
        @pl.loop(0, ny // 2, unroll=True)
        def _(n):
            start = pl.multiple_of(which * features + n * 2 * LANES, 2 * LANES)
            part = jnp.dot(
                mamba, wout[:, pl.ds(start, 2 * LANES)], preferred_element_type=F32
            )
            for q in range(PARTS):
                for h in range(2):
                    first = q * part_tokens + h * quarter
                    for j in range(2):
                        store(
                            q,
                            h,
                            2 * n + j,
                            part[first : first + quarter, j * LANES : (j + 1) * LANES],
                        )

    def into_opp(q, h, n, v):
        mx_opp[q, h, n] = v.astype(BF16)

    def into_r(q, h, n, v):
        if h == 0:
            mx_rc[q, n] = v
        else:
            mx_r[q, 1, n] = v.astype(BF16)

    def into_l(q, h, n, v):
        if h == 1:
            mx_lc[q, n] = v
        else:
            mx_l[q, 0, n] = v.astype(BF16)

    def into_own(q, h, n, v):
        mx_own[q, h, n] = v

    to_r, to_l = {"exp": xr}, {"exp": xl}

    def pass_on(side, q, h):
        held, device = (mx_r, to_r) if side == 0 else (mx_l, to_l)
        send(
            held.at[q, h], xn_recv.at[q, side, h], xn_ss.at[side], xn_rs.at[q], device,
        )

    def add_and_pass_on(q):
        arrived(xo_recv.at[q], xo_rs.at[q])
        mx_r[q, 0] = (mx_rc[q] + xo_recv[q, 0].astype(F32)).astype(BF16)
        pass_on(0, q, 0)
        mx_l[q, 1] = (mx_lc[q] + xo_recv[q, 1].astype(F32)).astype(BF16)
        pass_on(1, q, 1)

    project(xo, into_opp)
    for q in range(PARTS):
        send(mx_opp.at[q, 0], xo_recv.at[q, 0], xo_ss, xo_rs.at[q], to_r)
        send(mx_opp.at[q, 1], xo_recv.at[q, 1], xo_ss, xo_rs.at[q], to_l)
    project(xr, into_r)
    pass_on(0, 0, 1)
    project(xl, into_l)
    pass_on(1, 0, 0)
    for q in range(PARTS):
        add_and_pass_on(q)
        if q + 1 < PARTS:
            pass_on(0, q + 1, 1)
            pass_on(1, q + 1, 0)
        if q == 0:
            project(x, into_own)

    far_first = sorted(range(1, ny), key=lambda k: -min(k, ny - k))
    for q in range(PARTS):
        arrived(xn_recv.at[q], xn_rs.at[q])
        for n in range(ny):
            for h in range(2):
                ysend[q, n, h * quarter : (h + 1) * quarter, :] = (
                    mx_own[q, h, n]
                    + xn_recv[q, 0, h, n].astype(F32)
                    + xn_recv[q, 1, h, n].astype(F32)
                ).astype(BF16)
        for k in far_first:
            other = lax.rem(y + k, ny)
            send(
                ysend.at[q, other], yrecv.at[q, y], y_ss, y_rs.at[q],
                {"ch": other},
            )
        yrecv[q, y] = ysend[q, y]
    copy_resid.wait()
    streams = []
    for q in range(PARTS):
        arrived(yrecv.at[q, pl.ds(0, ny - 1)], y_rs.at[q])
        stream = resid[q * part_tokens : (q + 1) * part_tokens, :].astype(F32)
        for n in range(ny):
            stream = stream + yrecv[q, n].astype(F32)
        streams.append(stream)
    rows_of = jnp.concatenate(streams, axis=0).astype(BF16)

    main_rows = jnp.dot(pick_main[...], rows_of, preferred_element_type=F32).astype(BF16)
    tail_rows = jnp.dot(pick_tail[...], rows_of, preferred_element_type=F32)
    zm_send[...] = main_rows.reshape(wide_experts, MAIN_SLOTS, LANES)
    zt_send[...] = tail_rows.reshape(wide_experts, TAIL_SLOTS, LANES)

    def dispatch(owner):
        expert = lax.rem(owner, experts)
        device = {"seq": owner}
        send(zm_send.at[expert], zm_recv.at[s], zm_ss, zm_rs.at[s // sources], device)
        send(zt_send.at[expert], zt_recv.at[s], zt_ss, zt_rs.at[s // sources], device)

    dispatch(lax.rem(s + nz // 2, nz))

    @pl.loop(1, nz // 2)
    def _(k):
        far = nz // 2 - k
        dispatch(lax.rem(s + far, nz))
        dispatch(lax.rem(s + nz - far, nz))

    mine = lax.rem(s, experts)
    zm_recv[s] = zm_send[mine]
    zt_recv[s] = zt_send[mine]

    blocks = NX
    order = [xo, xr, xl, x]
    hops = ny // 2
    even = lax.rem(s, 2) == 0

    def fill(k):
        first = order[k] * sources

        def all_of(number):
            arrived(zm_recv.at[pl.ds(0, number)], zm_rs.at[order[k]])
            arrived(zt_recv.at[pl.ds(0, number)], zt_rs.at[order[k]])

        @pl.when(s // sources == order[k])
        def _():
            all_of(sources - 1)

        @pl.when(s // sources != order[k])
        def _():
            all_of(sources)

        ring[y, k, 0:main, :] = zm_recv[pl.ds(first, sources)].reshape(main, LANES)
        rest = zt_recv[pl.ds(first, sources)].reshape(tail, LANES)
        if tail < 16:
            rest = jnp.concatenate([rest, jnp.zeros((16 - tail, LANES), F32)], axis=0)
        ring[y, k, main:, :] = rest.astype(BF16)

    gated = pb_own.shape[-1]
    width = 256

    def prepare(k, n, first):
        v = ring[n, k].astype(F32)
        squares[k] = v * v if first else squares[k] + v * v
        at = pl.ds(pl.multiple_of(n * LANES, LANES), LANES)
        lhs[k, :, at] = (v * gain_ref[pl.ds(x * ny + n, 1), :]).astype(BF16)

    def expert_half(k, h, store):
        @pl.loop(0, gated // width, unroll=True)
        def _(n):
            start = pl.multiple_of(n * width, width)
            column = pl.multiple_of(h * gated + n * width, width)
            part = jnp.dot(
                lhs[k], wexp[:, pl.ds(column, width)], preferred_element_type=F32
            )
            store(h, pl.ds(start, width), part)

    def square_sums(k):
        sq_send[k] = lax.dot_general(
            jnp.ones((8, LANES), F32), squares[k], (((1,), (1,)), ((), ())),
            precision=EXACT, preferred_element_type=F32,
        )

    def keep_opp(h, at, v):
        pb_opp[h, :, at] = v.astype(BF16)

    def keep_r(h, at, v):
        if h == 0:
            pb_rc[:, at] = v
        else:
            pb_r[1, :, at] = v.astype(BF16)

    def keep_l(h, at, v):
        if h == 1:
            pb_lc[:, at] = v
        else:
            pb_l[0, :, at] = v.astype(BF16)

    def keep_own(h, at, v):
        pb_own[h, :, at] = v

    def all_left():
        arrived(s1h.at[pl.ds(0, STATE_GROUP - 1)], s1_ss.at[0])
        arrived(s1a.at[pl.ds(0, STATE_GROUP - 1)], s1_ss.at[1])
        for k in range(1, groups):

            @pl.when(group + k == groups - 1)
            def _():
                arrived(s2h.at[pl.ds(0, k)], s2_ss.at[0])
                arrived(s2a.at[pl.ds(0, k)], s2_ss.at[1])

        arrived(mx_opp, xo_ss)
        arrived(mx_r, xn_ss.at[0])
        arrived(mx_l, xn_ss.at[1])
        arrived(pb_opp, po_ss)
        arrived(ysend.at[:, pl.ds(0, ny - 1)], y_ss)
        arrived(sq_send.at[pl.ds(0, NX - 1)], sq_ss)

        arrived(zm_recv.at[pl.ds(0, nz - 1)], zm_ss)
        arrived(zt_recv.at[pl.ds(0, nz - 1)], zt_ss)
        arrived(ring.at[pl.ds(0, ny - 1)], ring_ss)

    def near(k):
        return lax.rem(y + ny + k, ny)

    def give(k, chunk, which, target):
        send(
            ring.at[chunk, k], ring.at[chunk, k], ring_ss, ring_rs.at[k, which],
            {"ch": near(target)},
        )

    def first_round_far(k):
        fill(k)
        if hops == 4:
            give(k, y, 0, 2)
            give(k, y, 1, -2)

    def first_round_near(k):
        if hops == 4:
            give(k, y, 2, 1)
            give(k, y, 2, -1)
        else:
            for other in far_first:
                give(k, y, 3, other)
        prepare(k, y, True)

    def first_round(k):
        first_round_far(k)
        first_round_near(k)

    def second_round(k):
        if hops == 4:
            arrived(ring.at[near(-2), k], ring_rs.at[k, 0])

            @pl.when(even)
            def _():
                give(k, near(-2), 3, 2)

            give(k, near(-2), 3, 1)
            arrived(ring.at[near(2), k], ring_rs.at[k, 1])

            @pl.when(jnp.logical_not(even))
            def _():
                give(k, near(2), 3, -2)

            give(k, near(2), 3, -1)
            prepare(k, near(-2), False)
            prepare(k, near(2), False)

    def neighbours_in(k):
        if hops == 4:
            arrived(ring.at[pl.ds(0, 2), k], ring_rs.at[k, 2])
            prepare(k, near(-1), False)
            prepare(k, near(1), False)

    def all_in(k):
        if hops == 4:
            arrived(ring.at[pl.ds(0, 3), k], ring_rs.at[k, 3])
            for other in (3, 4, 5):
                prepare(k, near(other), False)
        else:
            arrived(ring.at[pl.ds(0, ny - 1), k], ring_rs.at[k, 3])
            for other in range(1, ny):
                prepare(k, near(other), False)

    def opposite_half(turn):
        h = jnp.where(even, turn, 1 - turn)
        expert_half(0, h, keep_opp)
        device = {"exp": jnp.where(h == 0, xr, xl)}
        send(pb_opp.at[h], po_recv.at[h], po_ss, po_rs.at[h], device)

    first_round_far(0)
    first_round_near(0)
    first_round_far(1)
    second_round(0)
    first_round_near(1)
    neighbours_in(0)
    first_round(2)
    second_round(1)
    all_in(0)
    copy_wexp.wait()
    opposite_half(0)
    opposite_half(1)
    second_round(2)
    first_round(3)
    neighbours_in(1)
    all_in(1)
    expert_half(1, 1, keep_r)
    send(pb_r.at[1], pn_recv.at[0, 0], pn_ss.at[0], pn_rs.at[0], to_r)
    neighbours_in(2)
    all_in(2)
    expert_half(2, 0, keep_l)
    send(pb_l.at[0], pn_recv.at[0, 1], pn_ss.at[1], pn_rs.at[0], to_l)
    second_round(3)
    for k, device in enumerate(({"exp": xo}, to_r, to_l)):
        square_sums(k)
        send(sq_send.at[k], sq_recv.at[k], sq_ss, sq_rs, device)
    expert_half(1, 0, keep_r)
    expert_half(2, 1, keep_l)
    arrived(po_recv.at[0], po_rs.at[0])
    pb_r[0] = (pb_rc[...] + po_recv[0].astype(F32)).astype(BF16)
    send(pb_r.at[0], pn_recv.at[1, 0], pn_ss.at[0], pn_rs.at[1], to_r)
    arrived(po_recv.at[1], po_rs.at[1])
    pb_l[1] = (pb_lc[...] + po_recv[1].astype(F32)).astype(BF16)
    send(pb_l.at[1], pn_recv.at[1, 1], pn_ss.at[1], pn_rs.at[1], to_l)
    neighbours_in(3)
    all_in(3)
    square_sums(3)
    for h in range(2):
        expert_half(3, h, keep_own)

    all_left()
    arrived(sq_recv, sq_rs)
    sums = sq_send[3] + sq_recv[0] + sq_recv[1] + sq_recv[2]
    inverse = lax.rsqrt(sums / (NX * features) + EPSILON)
    scale = lax.dot_general(
        inverse, jnp.full((8, LANES), 0.125, F32), (((0,), (0,)), ((), ())),
        precision=EXACT, preferred_element_type=F32,
    )
    scale = jnp.concatenate([scale] * (width // LANES), axis=1)
    arrived(pn_recv.at[0], pn_rs.at[0])
    pb_own[1] = pb_own[1] + pn_recv[0, 0].astype(F32)
    pb_own[0] = pb_own[0] + pn_recv[0, 1].astype(F32)
    arrived(pn_recv.at[1], pn_rs.at[1])

    @pl.loop(0, gated // width, unroll=True)
    def _(n):
        at = pl.ds(pl.multiple_of(n * width, width), width)
        gate_part = scale * (pb_own[0, :, at] + pn_recv[1, 0, :, at].astype(F32))
        up_part = scale * (pb_own[1, :, at] + pn_recv[1, 1, :, at].astype(F32))
        hidden = (silu(gate_part) * up_part).astype(BF16)
        out_ref[:, at] = jnp.dot(
            arrange[...], hidden, preferred_element_type=F32
        ).astype(BF16)

    arrived(pb_r, pn_ss.at[0])
    arrived(pb_l, pn_ss.at[1])


def body(
    nz,
    ny,
    conv_x,
    gate_z,
    step,
    decay_rate,
    state_in,
    state_out,
    skip,
    out_weight,
    residual,
    norm_gain,
    expert_ids,
    expert_weights,
):
    tokens, channels = conv_x.shape
    entries = state_in.shape[1]
    features = expert_weights.shape[2]
    doubled = expert_weights.shape[-1]
    gated = doubled // 2
    part_tokens = tokens // PARTS
    quarter = part_tokens // 2
    sources = nz // NX
    tail = max(16, sources * TAIL_SLOTS)
    rows = sources * MAIN_SLOTS + tail
    experts = max(nz // 2, 16)
    hops = ny // 2
    groups = nz // STATE_GROUP
    dma = pltpu.SemaphoreType.DMA
    vmem = pltpu.VMEM
    scratch = [
        vmem((tokens, channels), BF16),
        vmem((tokens, channels), BF16),
        vmem((tokens, channels), BF16),
        vmem((channels // LANES, LANES), F32),
        vmem((entries, tokens), F32),
        vmem((entries, tokens), F32),
        vmem((channels // LANES, LANES), F32),
        vmem((norm_gain.shape[0] // LANES, LANES), F32),
        vmem((2, tokens), jnp.int32),
        vmem(out_weight.shape, BF16),
        vmem((tokens, LANES), BF16),
        vmem((features, doubled), BF16),
        vmem((tokens, channels), F32),
        vmem((tokens, channels), F32),
        vmem((tokens, channels), F32),
        vmem((tokens, channels), F32),
        vmem((STATE_GROUP, entries, channels), BF16),
        vmem((STATE_GROUP, 1, channels), F32),
        vmem((groups, entries, channels), BF16),
        vmem((groups, 1, channels), F32),
        vmem((entries, channels), F32),
        vmem((MAIN_SLOTS * experts, tokens), BF16),
        vmem((TAIL_SLOTS * experts, tokens), BF16),
        vmem((sources * (MAIN_SLOTS + TAIL_SLOTS), rows), BF16),
        vmem((PARTS, 2, ny, quarter, LANES), BF16),
        vmem((PARTS, 2, ny, quarter, LANES), BF16),
        vmem((PARTS, 2, ny, quarter, LANES), BF16),
        vmem((PARTS, ny, quarter, LANES), F32),
        vmem((PARTS, ny, quarter, LANES), F32),
        vmem((PARTS, 2, ny, quarter, LANES), F32),
        vmem((PARTS, 2, ny, quarter, LANES), BF16),
        vmem((PARTS, 2, 2, ny, quarter, LANES), BF16),
        vmem((PARTS, ny, part_tokens, LANES), BF16),
        vmem((PARTS, ny, part_tokens, LANES), BF16),
        vmem((experts, MAIN_SLOTS, LANES), BF16),
        vmem((experts, TAIL_SLOTS, LANES), F32),
        vmem((nz, MAIN_SLOTS, LANES), BF16),
        vmem((nz, TAIL_SLOTS, LANES), F32),
        vmem((ny, NX, rows, LANES), BF16),
        vmem((NX, rows, features), BF16),
        vmem((NX, rows, LANES), F32),
        vmem((2, rows, gated), BF16),
        vmem((2, rows, gated), BF16),
        vmem((2, rows, gated), BF16),
        vmem((rows, gated), F32),
        vmem((rows, gated), F32),
        vmem((2, rows, gated), F32),
        vmem((2, rows, gated), BF16),
        vmem((2, 2, rows, gated), BF16),
        vmem((NX, 8, rows), F32),
        vmem((NX - 1, 8, rows), F32),
        dma((12,)),
        dma((2,)),
        dma((2,)),
        dma((2,)),
        dma((2,)),
        dma,
        dma((PARTS,)),
        dma((2,)),
        dma((PARTS,)),
        dma,
        dma((PARTS,)),
        dma,
        dma((NX,)),
        dma,
        dma((NX,)),
        dma,
        dma((NX, 4)),
        dma,
        dma((2,)),
        dma((2,)),
        dma((2,)),
        dma,
        dma,
    ]
    whole = pl.BlockSpec(memory_space=pltpu.VMEM)
    far = pl.BlockSpec(memory_space=pl.ANY)
    out_rows = sources * (MAIN_SLOTS + TAIL_SLOTS)
    hidden = pl.pallas_call(
        functools.partial(kernel, nz, ny),
        out_shape=pltpu.VMEM((out_rows, gated), BF16),
        in_specs=[far] * 12,
        out_specs=whole,
        scratch_shapes=scratch,
        compiler_params=pltpu.CompilerParams(collective_id=0, has_side_effects=True),
        name="layer",
    )(
        conv_x,
        gate_z,
        step,
        decay_rate.reshape(channels // LANES, LANES),
        state_in.T,
        state_out.T,
        skip.reshape(channels // LANES, LANES),
        norm_gain.reshape(-1, LANES),
        expert_ids.T,
        out_weight,
        residual,
        expert_weights.reshape(features, doubled),
    )
    return hidden.reshape(1, out_rows, 1, gated)


def solution(mesh):
    in_specs = (
        P("seq", ("exp", "ch")),
        P("seq", ("exp", "ch")),
        P("seq", ("exp", "ch")),
        P(("exp", "ch")),
        P("seq", None),
        P("seq", None),
        P(("exp", "ch")),
        P(("exp", "ch"), None),
        P("seq", None),
        P(),
        P("seq", None),
        P("seq", None, "exp", "ch", None),
    )
    return jax.shard_map(
        functools.partial(body, mesh.shape["seq"], mesh.shape["ch"]),
        mesh=mesh,
        in_specs=in_specs,
        out_specs=P("seq", "exp", None, "ch"),
        check_vma=False,
    )
```

```python
import functools

import jax
import jax.numpy as jnp
from jax import lax
from jax.experimental import pallas as pl
from jax.experimental.pallas import tpu as pltpu
from jax.sharding import PartitionSpec as P

MESH = pl.DeviceIdType.MESH
F32 = jnp.float32
BF16 = jnp.bfloat16
EXACT = lax.Precision.HIGHEST
EPSILON = 1e-05
MAIN_SLOTS = 16
TAIL_SLOTS = 2
LANES = 128
STATE_GROUP = 4
NX = 4
PARTS = 8


def silu(v):
    return v / (1.0 + jnp.exp(-v))


def arrived(ref, sem):
    pltpu.make_async_copy(ref, ref, sem).wait()


def send(src, dst, send_sem, recv_sem, device):
    pltpu.make_async_remote_copy(
        src_ref=src,
        dst_ref=dst,
        send_sem=send_sem,
        recv_sem=recv_sem,
        device_id=device,
        device_id_type=MESH,
    ).start()


def kernel(
    nz,
    ny,
    conv_hbm,
    gate_hbm,
    step_hbm,
    rate_hbm,
    b_hbm,
    c_hbm,
    skip_hbm,
    gain_hbm,
    ids_hbm,
    wout_hbm,
    resid_hbm,
    wexp_hbm,
    out_ref,
    conv_ref,
    gate_ref,
    step_ref,
    rate_ref,
    b_ref,
    c_ref,
    skip_ref,
    gain_ref,
    ids_ref,
    wout,
    resid,
    wexp,
    e_ref,
    d_ref,
    y_ref,
    p_ref,
    s1h,
    s1a,
    s2h,
    s2a,
    inc_h,
    pick_main,
    pick_tail,
    arrange,
    mx_opp,
    mx_r,
    mx_l,
    mx_rc,
    mx_lc,
    mx_own,
    xo_recv,
    xn_recv,
    ysend,
    yrecv,
    zm_send,
    zt_send,
    zm_recv,
    zt_recv,
    ring,
    lhs,
    squares,
    pb_opp,
    pb_r,
    pb_l,
    pb_rc,
    pb_lc,
    pb_own,
    po_recv,
    pn_recv,
    sq_send,
    sq_recv,
    local_sem,
    s1_ss,
    s1_rs,
    s2_ss,
    s2_rs,
    xo_ss,
    xo_rs,
    xn_ss,
    xn_rs,
    y_ss,
    y_rs,
    zm_ss,
    zm_rs,
    zt_ss,
    zt_rs,
    ring_ss,
    ring_rs,
    po_ss,
    po_rs,
    pn_ss,
    pn_rs,
    sq_ss,
    sq_rs,
):
    s = lax.axis_index("seq")
    x = lax.axis_index("exp")
    y = lax.axis_index("ch")
    tokens, channels = conv_hbm.shape
    features = ny * LANES
    part_tokens = tokens // PARTS
    quarter = part_tokens // 2
    experts = nz // 2
    wide_experts = max(experts, 16)
    sources = nz // NX
    main = sources * MAIN_SLOTS
    tail = sources * TAIL_SLOTS
    block_rows = lhs.shape[1]
    xr, xl, xo = lax.rem(x + 1, NX), lax.rem(x + 3, NX), lax.rem(x + 2, NX)
    yr, yl = lax.rem(y + 1, ny), lax.rem(y + ny - 1, ny)

    share = pl.multiple_of((x * ny + y) * LANES, LANES)
    taken_in = [
        pltpu.make_async_copy(source, target, local_sem.at[k])
        for k, (source, target) in enumerate(
            (
                (step_hbm, step_ref),
                (rate_hbm, rate_ref),
                (conv_hbm, conv_ref),
                (b_hbm, b_ref),
                (c_hbm, c_ref),
                (gate_hbm, gate_ref),
                (skip_hbm, skip_ref),
                (ids_hbm, ids_ref),
                (gain_hbm, gain_ref),
                (wout_hbm, wout),
                (resid_hbm.at[:, pl.ds(share, LANES)], resid),
                (wexp_hbm, wexp),
            )
        )
    ]
    copy_wout, copy_resid, copy_wexp = taken_in[9:]
    for copy in taken_in[:5]:
        copy.start()

    barrier = pltpu.get_barrier_semaphore()

    def greet(device):
        pl.semaphore_signal(barrier, inc=1, device_id=device, device_id_type=MESH)

    greet({"seq": lax.rem(s + nz // 2, nz)})

    @pl.loop(1, nz // 2)
    def _(k):
        far = nz // 2 - k
        greet({"seq": lax.rem(s + far, nz)})
        greet({"seq": lax.rem(s + nz - far, nz)})

    for k in range(1, NX):
        greet({"exp": lax.rem(x + k, NX)})
    for k in range(1, ny):
        greet({"ch": lax.rem(y + k, ny)})
    for copy in taken_in[5:]:
        copy.start()
    for copy in taken_in[:5]:
        copy.wait()

    def wide(ref):
        return jnp.concatenate(
            [ref[k : k + 1, :] for k in range(channels // LANES)], axis=1
        )

    conv = conv_ref[...].astype(F32)
    decay_log = step_ref[...].astype(F32) * wide(rate_ref)
    decay = jnp.exp(-decay_log)
    twice = 2.0 * decay_log
    series = twice * (
        1.0
        - twice
        * (
            1.0 / 2.0
            - twice
            * (
                1.0 / 6.0
                - twice * (1.0 / 24.0 - twice * (1.0 / 120.0 - twice * (1.0 / 720.0)))
            )
        )
    )
    lost = jnp.where(twice < 0.25, series, 1.0 - jnp.exp(-twice))
    e_ref[...] = decay
    d_ref[...] = jnp.sqrt(lost) * conv

    def eight_tokens(i, carry):
        state, product, b_now, c_now = carry
        rows = pl.ds(pl.multiple_of(i * 8, 8), 8)
        e8 = e_ref[rows, :]
        d8 = d_ref[rows, :]
        outs, products = [], []
        for k in range(8):
            e1 = e8[k : k + 1, :]
            state = e1 * state + d8[k : k + 1, :] * b_now[:, k : k + 1]
            product = product * e1
            outs.append(jnp.sum(state * c_now[:, k : k + 1], axis=0, keepdims=True))
            products.append(product)
        y_ref[rows, :] = jnp.concatenate(outs, axis=0)
        p_ref[rows, :] = jnp.concatenate(products, axis=0)
        shift = b_now.shape[1] - 8
        return state, product, pltpu.roll(b_now, shift, 1), pltpu.roll(c_now, shift, 1)

    state, product, _, _ = lax.fori_loop(
        0,
        tokens // 8,
        eight_tokens,
        (
            jnp.zeros((b_ref.shape[0], channels), F32),
            jnp.ones((1, channels), F32),
            b_ref[...],
            c_ref[...],
        ),
    )

    group, place = s // STATE_GROUP, lax.rem(s, STATE_GROUP)
    groups = nz // STATE_GROUP
    s1h[place] = state.astype(BF16)
    s1a[place] = product
    pl.semaphore_wait(barrier, nz - 1 + NX - 1 + ny - 1)
    for k in range(1, STATE_GROUP):
        other = lax.rem(place + k, STATE_GROUP)
        device = {"seq": group * STATE_GROUP + other}
        send(s1h.at[place], s1h.at[place], s1_ss.at[0], s1_rs.at[0], device)
        send(s1a.at[place], s1a.at[place], s1_ss.at[1], s1_rs.at[1], device)
    for copy in taken_in[5:9]:
        copy.wait()
    gates = silu(gate_ref[...].astype(F32))
    within = y_ref[...] + wide(skip_ref) * conv
    arrived(s1h.at[pl.ds(0, STATE_GROUP - 1)], s1_rs.at[0])
    arrived(s1a.at[pl.ds(0, STATE_GROUP - 1)], s1_rs.at[1])
    total_h = jnp.zeros_like(state)
    total_a = jnp.ones_like(product)
    before_h = jnp.zeros_like(state)
    before_a = jnp.ones_like(product)
    for j in range(STATE_GROUP):
        h_j = s1h[j].astype(F32)
        a_j = s1a[j]
        total_h = a_j * total_h + h_j
        total_a = a_j * total_a
        earlier = j < place
        before_h = jnp.where(earlier, a_j * before_h + h_j, before_h)
        before_a = jnp.where(earlier, a_j * before_a, before_a)
    s2h[group] = total_h.astype(BF16)
    s2a[group] = total_a
    for k in range(groups - 1, 0, -1):

        @pl.when(group + k < groups)
        def _():
            device = {"seq": s + k * STATE_GROUP}
            send(s2h.at[group], s2h.at[group], s2_ss.at[0], s2_rs.at[0], device)
            send(s2a.at[group], s2a.at[group], s2_ss.at[1], s2_rs.at[1], device)

    names = lax.broadcasted_iota(jnp.int32, (wide_experts, tokens), 0)
    named = (ids_ref[0:1, :] == names) | (ids_ref[1:2, :] == names)
    count = jnp.where(named, 1.0, 0.0)
    before = jnp.where(
        lax.broadcasted_iota(jnp.int32, (tokens, tokens), 0)
        < lax.broadcasted_iota(jnp.int32, (tokens, tokens), 1),
        1.0,
        0.0,
    )
    earlier = jnp.dot(
        count.astype(BF16), before.astype(BF16), preferred_element_type=F32
    )
    slot = jnp.where(named, earlier, -1.0).astype(BF16)

    def picked(slots, first):
        rows = slots * wide_experts
        spread = jnp.where(
            lax.broadcasted_iota(jnp.int32, (rows, wide_experts), 0) // slots
            == lax.broadcasted_iota(jnp.int32, (rows, wide_experts), 1),
            1.0,
            0.0,
        ).astype(BF16)
        per_row = jnp.dot(spread, slot, preferred_element_type=F32)
        wanted = lax.rem(
            lax.broadcasted_iota(jnp.int32, (rows, tokens), 0), slots
        ).astype(F32) + float(first)
        return jnp.where(per_row == wanted, 1.0, 0.0).astype(BF16)

    pick_main[...] = picked(MAIN_SLOTS, 0)
    pick_tail[...] = picked(TAIL_SLOTS, MAIN_SLOTS)
    slots = MAIN_SLOTS + TAIL_SLOTS
    final = lax.broadcasted_iota(jnp.int32, (sources * slots, block_rows), 0)
    place_of = lax.broadcasted_iota(jnp.int32, (sources * slots, block_rows), 1)
    owner_row, slot_row = final // slots, lax.rem(final, slots)
    taken = jnp.where(
        slot_row < MAIN_SLOTS,
        owner_row * MAIN_SLOTS + slot_row,
        main + owner_row * TAIL_SLOTS + slot_row - MAIN_SLOTS,
    )
    arrange[...] = jnp.where(taken == place_of, 1.0, 0.0).astype(BF16)

    inc_h[...] = jnp.zeros_like(state)
    for j in range(1, groups):

        @pl.when(j == group)
        def _():
            arrived(s2h.at[pl.ds(0, j)], s2_rs.at[0])
            arrived(s2a.at[pl.ds(0, j)], s2_rs.at[1])

    for j in range(groups - 1):

        @pl.when(j < group)
        def _():
            inc_h[...] = s2a[j] * inc_h[...] + s2h[j].astype(F32)

    incoming = before_a * inc_h[...] + before_h

    carried = lax.dot_general(
        c_ref[...], incoming, (((0,), (0,)), ((), ())), precision=EXACT,
        preferred_element_type=F32,
    )
    mamba = ((within + p_ref[...] * carried) * gates).astype(BF16)
    copy_wout.wait()

    def project(which, store):
        @pl.loop(0, ny // 2, unroll=True)
        def _(n):
            start = pl.multiple_of(which * features + n * 2 * LANES, 2 * LANES)
            part = jnp.dot(
                mamba, wout[:, pl.ds(start, 2 * LANES)], preferred_element_type=F32
            )
            for q in range(PARTS):
                for h in range(2):
                    first = q * part_tokens + h * quarter
                    for j in range(2):
                        store(
                            q,
                            h,
                            2 * n + j,
                            part[first : first + quarter, j * LANES : (j + 1) * LANES],
                        )

    def into_opp(q, h, n, v):
        mx_opp[q, h, n] = v.astype(BF16)

    def into_r(q, h, n, v):
        if h == 0:
            mx_rc[q, n] = v
        else:
            mx_r[q, 1, n] = v.astype(BF16)

    def into_l(q, h, n, v):
        if h == 1:
            mx_lc[q, n] = v
        else:
            mx_l[q, 0, n] = v.astype(BF16)

    def into_own(q, h, n, v):
        mx_own[q, h, n] = v

    to_r, to_l = {"exp": xr}, {"exp": xl}

    def pass_on(side, q, h):
        held, device = (mx_r, to_r) if side == 0 else (mx_l, to_l)
        send(
            held.at[q, h], xn_recv.at[q, side, h], xn_ss.at[side], xn_rs.at[q], device,
        )

    def add_and_pass_on(q):
        arrived(xo_recv.at[q], xo_rs.at[q])
        mx_r[q, 0] = (mx_rc[q] + xo_recv[q, 0].astype(F32)).astype(BF16)
        pass_on(0, q, 0)
        mx_l[q, 1] = (mx_lc[q] + xo_recv[q, 1].astype(F32)).astype(BF16)
        pass_on(1, q, 1)

    project(xo, into_opp)
    for q in range(PARTS):
        send(mx_opp.at[q, 0], xo_recv.at[q, 0], xo_ss, xo_rs.at[q], to_r)
        send(mx_opp.at[q, 1], xo_recv.at[q, 1], xo_ss, xo_rs.at[q], to_l)
    project(xr, into_r)
    pass_on(0, 0, 1)
    project(xl, into_l)
    pass_on(1, 0, 0)
    for q in range(PARTS):
        add_and_pass_on(q)
        if q + 1 < PARTS:
            pass_on(0, q + 1, 1)
            pass_on(1, q + 1, 0)
        if q == 0:
            project(x, into_own)

    far_first = sorted(range(1, ny), key=lambda k: -min(k, ny - k))
    for q in range(PARTS):
        arrived(xn_recv.at[q], xn_rs.at[q])
        for n in range(ny):
            for h in range(2):
                ysend[q, n, h * quarter : (h + 1) * quarter, :] = (
                    mx_own[q, h, n]
                    + xn_recv[q, 0, h, n].astype(F32)
                    + xn_recv[q, 1, h, n].astype(F32)
                ).astype(BF16)
        for k in far_first:
            other = lax.rem(y + k, ny)
            send(
                ysend.at[q, other], yrecv.at[q, y], y_ss, y_rs.at[q],
                {"ch": other},
            )
        yrecv[q, y] = ysend[q, y]
    copy_resid.wait()
    streams = []
    for q in range(PARTS):
        arrived(yrecv.at[q, pl.ds(0, ny - 1)], y_rs.at[q])
        stream = resid[q * part_tokens : (q + 1) * part_tokens, :].astype(F32)
        for n in range(ny):
            stream = stream + yrecv[q, n].astype(F32)
        streams.append(stream)
    rows_of = jnp.concatenate(streams, axis=0).astype(BF16)

    main_rows = jnp.dot(pick_main[...], rows_of, preferred_element_type=F32).astype(BF16)
    tail_rows = jnp.dot(pick_tail[...], rows_of, preferred_element_type=F32)
    zm_send[...] = main_rows.reshape(wide_experts, MAIN_SLOTS, LANES)
    zt_send[...] = tail_rows.reshape(wide_experts, TAIL_SLOTS, LANES)

    def dispatch(owner):
        expert = lax.rem(owner, experts)
        device = {"seq": owner}
        send(zm_send.at[expert], zm_recv.at[s], zm_ss, zm_rs.at[s // sources], device)
        send(zt_send.at[expert], zt_recv.at[s], zt_ss, zt_rs.at[s // sources], device)

    dispatch(lax.rem(s + nz // 2, nz))

    @pl.loop(1, nz // 2)
    def _(k):
        far = nz // 2 - k
        dispatch(lax.rem(s + far, nz))
        dispatch(lax.rem(s + nz - far, nz))

    mine = lax.rem(s, experts)
    zm_recv[s] = zm_send[mine]
    zt_recv[s] = zt_send[mine]

    blocks = NX
    order = [xo, xr, xl, x]
    hops = ny // 2
    even = lax.rem(s, 2) == 0

    def fill(k):
        first = order[k] * sources

        def all_of(number):
            arrived(zm_recv.at[pl.ds(0, number)], zm_rs.at[order[k]])
            arrived(zt_recv.at[pl.ds(0, number)], zt_rs.at[order[k]])

        @pl.when(s // sources == order[k])
        def _():
            all_of(sources - 1)

        @pl.when(s // sources != order[k])
        def _():
            all_of(sources)

        ring[y, k, 0:main, :] = zm_recv[pl.ds(first, sources)].reshape(main, LANES)
        rest = zt_recv[pl.ds(first, sources)].reshape(tail, LANES)
        if tail < 16:
            rest = jnp.concatenate([rest, jnp.zeros((16 - tail, LANES), F32)], axis=0)
        ring[y, k, main:, :] = rest.astype(BF16)

    gated = pb_own.shape[-1]
    width = 256

    def prepare(k, n, first):
        v = ring[n, k].astype(F32)
        squares[k] = v * v if first else squares[k] + v * v
        at = pl.ds(pl.multiple_of(n * LANES, LANES), LANES)
        lhs[k, :, at] = (v * gain_ref[pl.ds(x * ny + n, 1), :]).astype(BF16)

    def expert_half(k, h, store):
        @pl.loop(0, gated // width, unroll=True)
        def _(n):
            start = pl.multiple_of(n * width, width)
            column = pl.multiple_of(h * gated + n * width, width)
            part = jnp.dot(
                lhs[k], wexp[:, pl.ds(column, width)], preferred_element_type=F32
            )
            store(h, pl.ds(start, width), part)

    def square_sums(k):
        sq_send[k] = lax.dot_general(
            jnp.ones((8, LANES), F32), squares[k], (((1,), (1,)), ((), ())),
            precision=EXACT, preferred_element_type=F32,
        )

    def keep_opp(h, at, v):
        pb_opp[h, :, at] = v.astype(BF16)

    def keep_r(h, at, v):
        if h == 0:
            pb_rc[:, at] = v
        else:
            pb_r[1, :, at] = v.astype(BF16)

    def keep_l(h, at, v):
        if h == 1:
            pb_lc[:, at] = v
        else:
            pb_l[0, :, at] = v.astype(BF16)

    def keep_own(h, at, v):
        pb_own[h, :, at] = v

    def all_left():
        arrived(s1h.at[pl.ds(0, STATE_GROUP - 1)], s1_ss.at[0])
        arrived(s1a.at[pl.ds(0, STATE_GROUP - 1)], s1_ss.at[1])
        for k in range(1, groups):

            @pl.when(group + k == groups - 1)
            def _():
                arrived(s2h.at[pl.ds(0, k)], s2_ss.at[0])
                arrived(s2a.at[pl.ds(0, k)], s2_ss.at[1])

        arrived(mx_opp, xo_ss)
        arrived(mx_r, xn_ss.at[0])
        arrived(mx_l, xn_ss.at[1])
        arrived(pb_opp, po_ss)
        arrived(ysend.at[:, pl.ds(0, ny - 1)], y_ss)
        arrived(sq_send.at[pl.ds(0, NX - 1)], sq_ss)

        arrived(zm_recv.at[pl.ds(0, nz - 1)], zm_ss)
        arrived(zt_recv.at[pl.ds(0, nz - 1)], zt_ss)
        arrived(ring.at[pl.ds(0, ny - 1)], ring_ss)

    def near(k):
        return lax.rem(y + ny + k, ny)

    def give(k, chunk, which, target):
        send(
            ring.at[chunk, k], ring.at[chunk, k], ring_ss, ring_rs.at[k, which],
            {"ch": near(target)},
        )

    def first_round_far(k):
        fill(k)
        if hops == 4:
            give(k, y, 0, 2)
            give(k, y, 1, -2)

    def first_round_near(k):
        if hops == 4:
            give(k, y, 2, 1)
            give(k, y, 2, -1)
        else:
            for other in far_first:
                give(k, y, 3, other)
        prepare(k, y, True)

    def first_round(k):
        first_round_far(k)
        first_round_near(k)

    def second_round(k):
        if hops == 4:
            arrived(ring.at[near(-2), k], ring_rs.at[k, 0])

            @pl.when(even)
            def _():
                give(k, near(-2), 3, 2)

            give(k, near(-2), 3, 1)
            arrived(ring.at[near(2), k], ring_rs.at[k, 1])

            @pl.when(jnp.logical_not(even))
            def _():
                give(k, near(2), 3, -2)

            give(k, near(2), 3, -1)
            prepare(k, near(-2), False)
            prepare(k, near(2), False)

    def neighbours_in(k):
        if hops == 4:
            arrived(ring.at[pl.ds(0, 2), k], ring_rs.at[k, 2])
            prepare(k, near(-1), False)
            prepare(k, near(1), False)

    def all_in(k):
        if hops == 4:
            arrived(ring.at[pl.ds(0, 3), k], ring_rs.at[k, 3])
            for other in (3, 4, 5):
                prepare(k, near(other), False)
        else:
            arrived(ring.at[pl.ds(0, ny - 1), k], ring_rs.at[k, 3])
            for other in range(1, ny):
                prepare(k, near(other), False)

    def opposite_half(turn):
        h = jnp.where(even, turn, 1 - turn)
        expert_half(0, h, keep_opp)
        device = {"exp": jnp.where(h == 0, xr, xl)}
        send(pb_opp.at[h], po_recv.at[h], po_ss, po_rs.at[h], device)

    first_round_far(0)
    first_round_near(0)
    first_round_far(1)
    second_round(0)
    first_round_near(1)
    neighbours_in(0)
    first_round(2)
    second_round(1)
    all_in(0)
    copy_wexp.wait()
    opposite_half(0)
    opposite_half(1)
    second_round(2)
    first_round(3)
    neighbours_in(1)
    all_in(1)
    expert_half(1, 1, keep_r)
    send(pb_r.at[1], pn_recv.at[0, 0], pn_ss.at[0], pn_rs.at[0], to_r)
    neighbours_in(2)
    all_in(2)
    expert_half(2, 0, keep_l)
    send(pb_l.at[0], pn_recv.at[0, 1], pn_ss.at[1], pn_rs.at[0], to_l)
    second_round(3)
    for k, device in enumerate(({"exp": xo}, to_r, to_l)):
        square_sums(k)
        send(sq_send.at[k], sq_recv.at[k], sq_ss, sq_rs, device)
    expert_half(1, 0, keep_r)
    expert_half(2, 1, keep_l)
    arrived(po_recv.at[0], po_rs.at[0])
    pb_r[0] = (pb_rc[...] + po_recv[0].astype(F32)).astype(BF16)
    send(pb_r.at[0], pn_recv.at[1, 0], pn_ss.at[0], pn_rs.at[1], to_r)
    arrived(po_recv.at[1], po_rs.at[1])
    pb_l[1] = (pb_lc[...] + po_recv[1].astype(F32)).astype(BF16)
    send(pb_l.at[1], pn_recv.at[1, 1], pn_ss.at[1], pn_rs.at[1], to_l)
    neighbours_in(3)
    all_in(3)
    square_sums(3)
    for h in range(2):
        expert_half(3, h, keep_own)

    all_left()
    arrived(sq_recv, sq_rs)
    sums = sq_send[3] + sq_recv[0] + sq_recv[1] + sq_recv[2]
    inverse = lax.rsqrt(sums / (NX * features) + EPSILON)
    scale = lax.dot_general(
        inverse, jnp.full((8, LANES), 0.125, F32), (((0,), (0,)), ((), ())),
        precision=EXACT, preferred_element_type=F32,
    )
    scale = jnp.concatenate([scale] * (width // LANES), axis=1)
    arrived(pn_recv.at[0], pn_rs.at[0])
    pb_own[1] = pb_own[1] + pn_recv[0, 0].astype(F32)
    pb_own[0] = pb_own[0] + pn_recv[0, 1].astype(F32)
    arrived(pn_recv.at[1], pn_rs.at[1])

    @pl.loop(0, gated // width, unroll=True)
    def _(n):
        at = pl.ds(pl.multiple_of(n * width, width), width)
        gate_part = scale * (pb_own[0, :, at] + pn_recv[1, 0, :, at].astype(F32))
        up_part = scale * (pb_own[1, :, at] + pn_recv[1, 1, :, at].astype(F32))
        hidden = (silu(gate_part) * up_part).astype(BF16)
        out_ref[:, at] = jnp.dot(
            arrange[...], hidden, preferred_element_type=F32
        ).astype(BF16)

    arrived(pb_r, pn_ss.at[0])
    arrived(pb_l, pn_ss.at[1])


def body(
    nz,
    ny,
    conv_x,
    gate_z,
    step,
    decay_rate,
    state_in,
    state_out,
    skip,
    out_weight,
    residual,
    norm_gain,
    expert_ids,
    expert_weights,
):
    tokens, channels = conv_x.shape
    entries = state_in.shape[1]
    features = expert_weights.shape[2]
    doubled = expert_weights.shape[-1]
    gated = doubled // 2
    part_tokens = tokens // PARTS
    quarter = part_tokens // 2
    sources = nz // NX
    tail = max(16, sources * TAIL_SLOTS)
    rows = sources * MAIN_SLOTS + tail
    experts = max(nz // 2, 16)
    hops = ny // 2
    groups = nz // STATE_GROUP
    dma = pltpu.SemaphoreType.DMA
    vmem = pltpu.VMEM
    scratch = [
        vmem((tokens, channels), BF16),
        vmem((tokens, channels), BF16),
        vmem((tokens, channels), BF16),
        vmem((channels // LANES, LANES), F32),
        vmem((entries, tokens), F32),
        vmem((entries, tokens), F32),
        vmem((channels // LANES, LANES), F32),
        vmem((norm_gain.shape[0] // LANES, LANES), F32),
        vmem((2, tokens), jnp.int32),
        vmem(out_weight.shape, BF16),
        vmem((tokens, LANES), BF16),
        vmem((features, doubled), BF16),
        vmem((tokens, channels), F32),
        vmem((tokens, channels), F32),
        vmem((tokens, channels), F32),
        vmem((tokens, channels), F32),
        vmem((STATE_GROUP, entries, channels), BF16),
        vmem((STATE_GROUP, 1, channels), F32),
        vmem((groups, entries, channels), BF16),
        vmem((groups, 1, channels), F32),
        vmem((entries, channels), F32),
        vmem((MAIN_SLOTS * experts, tokens), BF16),
        vmem((TAIL_SLOTS * experts, tokens), BF16),
        vmem((sources * (MAIN_SLOTS + TAIL_SLOTS), rows), BF16),
        vmem((PARTS, 2, ny, quarter, LANES), BF16),
        vmem((PARTS, 2, ny, quarter, LANES), BF16),
        vmem((PARTS, 2, ny, quarter, LANES), BF16),
        vmem((PARTS, ny, quarter, LANES), F32),
        vmem((PARTS, ny, quarter, LANES), F32),
        vmem((PARTS, 2, ny, quarter, LANES), F32),
        vmem((PARTS, 2, ny, quarter, LANES), BF16),
        vmem((PARTS, 2, 2, ny, quarter, LANES), BF16),
        vmem((PARTS, ny, part_tokens, LANES), BF16),
        vmem((PARTS, ny, part_tokens, LANES), BF16),
        vmem((experts, MAIN_SLOTS, LANES), BF16),
        vmem((experts, TAIL_SLOTS, LANES), F32),
        vmem((nz, MAIN_SLOTS, LANES), BF16),
        vmem((nz, TAIL_SLOTS, LANES), F32),
        vmem((ny, NX, rows, LANES), BF16),
        vmem((NX, rows, features), BF16),
        vmem((NX, rows, LANES), F32),
        vmem((2, rows, gated), BF16),
        vmem((2, rows, gated), BF16),
        vmem((2, rows, gated), BF16),
        vmem((rows, gated), F32),
        vmem((rows, gated), F32),
        vmem((2, rows, gated), F32),
        vmem((2, rows, gated), BF16),
        vmem((2, 2, rows, gated), BF16),
        vmem((NX, 8, rows), F32),
        vmem((NX - 1, 8, rows), F32),
        dma((12,)),
        dma((2,)),
        dma((2,)),
        dma((2,)),
        dma((2,)),
        dma,
        dma((PARTS,)),
        dma((2,)),
        dma((PARTS,)),
        dma,
        dma((PARTS,)),
        dma,
        dma((NX,)),
        dma,
        dma((NX,)),
        dma,
        dma((NX, 4)),
        dma,
        dma((2,)),
        dma((2,)),
        dma((2,)),
        dma,
        dma,
    ]
    whole = pl.BlockSpec(memory_space=pltpu.VMEM)
    far = pl.BlockSpec(memory_space=pl.ANY)
    out_rows = sources * (MAIN_SLOTS + TAIL_SLOTS)
    hidden = pl.pallas_call(
        functools.partial(kernel, nz, ny),
        out_shape=pltpu.VMEM((out_rows, gated), BF16),
        in_specs=[far] * 12,
        out_specs=whole,
        scratch_shapes=scratch,
        compiler_params=pltpu.CompilerParams(collective_id=0, has_side_effects=True),
        name="layer",
    )(
        conv_x,
        gate_z,
        step,
        decay_rate.reshape(channels // LANES, LANES),
        state_in.T,
        state_out.T,
        skip.reshape(channels // LANES, LANES),
        norm_gain.reshape(-1, LANES),
        expert_ids.T,
        out_weight,
        residual,
        expert_weights.reshape(features, doubled),
    )
    return hidden.reshape(1, out_rows, 1, gated)


def solution(mesh):
    in_specs = (
        P("seq", ("exp", "ch")),
        P("seq", ("exp", "ch")),
        P("seq", ("exp", "ch")),
        P(("exp", "ch")),
        P("seq", None),
        P("seq", None),
        P(("exp", "ch")),
        P(("exp", "ch"), None),
        P("seq", None),
        P(),
        P("seq", None),
        P("seq", None, "exp", "ch", None),
    )
    return jax.shard_map(
        functools.partial(body, mesh.shape["seq"], mesh.shape["ch"]),
        mesh=mesh,
        in_specs=in_specs,
        out_specs=P("seq", "exp", None, "ch"),
        check_vma=False,
    )
```
